512 devices in a mesh: rows: 128 (over x, z, core), rhs: 4 (over y).
Axes of the slice: x: 4, y: 4, z: 16, core: 2. Of those that a mesh axis runs over, the one named last changes fastest.
Arguments:
- targets: float32 [32768, 1024], P(('rows', 'rhs')), may hold values from -6 to 6
- send_order: int32 [32768], P('rows'), may hold values from 0 to 255, as said below
- send_count: int32 [128, 128], P('rows'), may hold values from 0 to 4, as said below
- recv_slot: int32 [32768], P('rows'), may hold values from 0 to 255, as said below
- panel: float32 [32768, 4096], P('rows'), may hold values from -0.09375 to 0.09375
- inv_diag: float32 [4, 1024, 1024], P(None, None, 'rows'), may hold values from -0.075 to 1.4, as said below
Outputs:
- solution: float32 [32768, 1024], P('rows', 'rhs')
The draws below stay inside these ranges and needn't reach their ends.
Inputs may be any that keep to these rules, and one draw needn't show every extreme that they name: For each rows index a, send_order[a * 256 : (a + 1) * 256] is a permutation of 0 .. 255 whose destinations (as the steps define them) do not fall. Each row and each column of send_count sums to 256; some entry equals 4. There are a permutation p of the rows indices and a table h with send_count[a, p(j)] = h[(j - a) mod 128]. `recv_slot`: every rows index receives each slot 0 .. 255 exactly once. Each inv_diag[k] is lower triangular with diagonal entries from 0.6 to 1.4 and entries below the diagonal within -0.075 to 0.075.
All inputs are finite; a program needn't handle non-finite values.
Results may differ from the reference program's by a relative error of at most 0.0001.
Values sent between devices are 32-bit elements; how exact they have to be, the bound alone decides.
No kernel may reach another device: no remote copies, remote signals or barrier semaphores. Data moves between devices by JAX's collectives and lax.ppermute only.
A program may use at most 64 MiB of HBM per device.

```python
import jax
import jax.numpy as jnp
from jax import lax

BS = 1024
NB = 4
C = 1024
W = 4096
OWN = 8
RD = 256
M = 32768
N_ROWS = 128


def routing_tables(key):
    folded = jax.random.fold_in(key, 1013)
    subkeys = jax.random.split(folded, 5)
    groups = M // RD
    mean_rows = RD // groups
    leftover = RD % groups
    spread = jax.random.randint(subkeys[0], (groups // 2,), 0, mean_rows + 1, dtype=jnp.int32)
    spread = spread.at[0].set(mean_rows)
    group_sizes = jnp.stack([mean_rows + spread, mean_rows - spread], axis=1).reshape(groups)
    group_sizes = group_sizes + (jnp.arange(groups, dtype=jnp.int32) < leftover).astype(jnp.int32)
    offsets = jnp.cumsum(group_sizes) - group_sizes
    shifts = jax.random.permutation(subkeys[1], groups).astype(jnp.int32)
    relabel = jax.random.permutation(subkeys[2], groups).astype(jnp.int32)
    slot_perm = jax.random.permutation(subkeys[3], RD).astype(jnp.int32)
    local_perm = jax.vmap(lambda item: jax.random.permutation(item, RD))(jax.random.split(subkeys[4], groups)).astype(jnp.int32)
    position = jnp.arange(RD, dtype=jnp.int32)
    member = jnp.sum((offsets[None, :] <= position[:, None]).astype(jnp.int32), axis=1) - 1
    source = jnp.arange(groups, dtype=jnp.int32)
    target_of = relabel[(source[:, None] + shifts[member][None, :]) % groups]
    inverse_local = jnp.argsort(local_perm, axis=1)
    slot_table = slot_perm[inverse_local].astype(jnp.int32)
    sort_key = target_of * RD + position[None, :]
    order_table = jnp.take_along_axis(local_perm, jnp.argsort(sort_key, axis=1), axis=1).astype(jnp.int32)
    receivers = relabel[(source[:, None] + shifts[None, :]) % groups]
    count_table = jnp.zeros((groups, groups), jnp.int32).at[jnp.broadcast_to(source[:, None], (groups, groups)), receivers].add(jnp.broadcast_to(group_sizes[None, :], (groups, groups)))
    return (order_table, count_table, slot_table)


def draw_send_order(key, part):
    order_table, count_table, slot_table = routing_tables(key)
    return order_table.reshape(-1)


def draw_send_count(key, part):
    order_table, count_table, slot_table = routing_tables(key)
    return count_table


def draw_recv_slot(key, part):
    order_table, count_table, slot_table = routing_tables(key)
    return slot_table.reshape(-1)


def draw_inv_diag(key, part):
    subkeys = jax.random.split(jax.random.fold_in(key, 2027), 2)
    row_index = jnp.arange(BS)[:, None]
    col_index = jnp.arange(BS)[None, :]
    below = (row_index > col_index).astype(jnp.float32)
    on_diag = (row_index == col_index).astype(jnp.float32)
    coupling = jnp.clip(jax.random.normal(subkeys[0], (NB, BS, BS), jnp.float32), -4.0, 4.0)
    pivots = jax.random.uniform(subkeys[1], (NB, BS, 1), jnp.float32, 0.6, 1.4)
    return coupling * 0.01875 * below + pivots * on_diag


def levels(own_key, shape, pieces, smallest, high):
    factor_of = 1.0
    for dim, parts in pieces:
        heights = jax.random.uniform(jax.random.fold_in(jax.random.fold_in(own_key, 6), dim), (parts,), jnp.float32, smallest / len(pieces), high / len(pieces))
        factor_of = factor_of * jnp.repeat(jnp.exp(heights), shape[dim] // parts).reshape((-1,) + (1,) * (len(shape) - 1 - dim))
    return factor_of


def bell_draw(stream_key, dims, deviation, limit, pieces=(), held_as=jnp.bfloat16):
    values = jax.random.normal(stream_key, dims, jnp.float32) * deviation
    if len(pieces) > 0:
        values = levels(stream_key, dims, pieces, -0.22, 0.18) * values
    return jnp.clip(values, min=-limit, max=limit).astype(held_as)


def setup_inputs(seed: int = 0) -> dict:
    seeds = jax.random.split(jax.random.key(seed), 7)
    return {
        "targets": bell_draw(seeds[0], (M, C), 1.0, 6.0, ((0, 512),), jnp.float32),
        "send_order": draw_send_order(jax.random.fold_in(seeds[6], 71), 0),
        "send_count": draw_send_count(jax.random.fold_in(seeds[6], 71), 0),
        "recv_slot": draw_recv_slot(jax.random.fold_in(seeds[6], 71), 0),
        "panel": bell_draw(seeds[4], (M, W), (NB * BS) ** -0.5, 0.09375, ((0, 128),), jnp.float32),
        "inv_diag": draw_inv_diag(jax.random.fold_in(seeds[6], 71), 0),
    }


def destinations(send_order, send_count):
    listing = send_order.reshape(N_ROWS, RD)
    position = jnp.argsort(listing, axis=1).astype(jnp.int32)
    bounds = jnp.cumsum(send_count, axis=1).astype(jnp.int32)
    passed = (bounds[:, None, :] <= position[:, :, None]).astype(jnp.int32)
    return jnp.sum(passed, axis=2).astype(jnp.int32)


def reference(targets, send_order, send_count, recv_slot, panel, inv_diag):
    target_dest = destinations(send_order, send_count)
    held_index = (target_dest * RD + recv_slot.reshape(N_ROWS, RD).astype(jnp.int32)).reshape(-1).astype(jnp.int32)
    arrived = jnp.zeros(targets.shape, jnp.float32).at[held_index].set(targets)
    residual = arrived.reshape(N_ROWS, RD, C)
    stacked = panel.reshape(N_ROWS, RD, NB * BS)
    outputs = []
    for section_index in range(NB):
        pending = residual[:, section_index * OWN:(section_index + 1) * OWN, :].reshape(BS, C)
        solved = jnp.dot(inv_diag[section_index], pending, precision=lax.Precision.HIGHEST, preferred_element_type=jnp.float32)
        outputs.append(solved.reshape(N_ROWS, OWN, C))
        first_live = (section_index + 1) * OWN
        factor_rows = stacked[:, first_live:, section_index * BS:(section_index + 1) * BS].reshape(-1, BS)
        change = jnp.dot(factor_rows, solved, precision=lax.Precision.HIGHEST, preferred_element_type=jnp.float32)
        residual = jnp.concatenate([residual[:, :first_live], residual[:, first_live:] - change.reshape(N_ROWS, RD - first_live, C)], axis=1)
    result = jnp.concatenate(outputs + [residual[:, NB * OWN:]], axis=1)
    return result.reshape(N_ROWS * RD, C)
```

```python
import jax
import jax.numpy as jnp
from jax import lax
from jax.sharding import Mesh, PartitionSpec as P

ROWS = ("x", "z", "core")


def product(left, right):
    return jnp.dot(left, right, precision=lax.Precision.HIGHEST, preferred_element_type=jnp.float32)


def gather_axis(block, axis):
    copies = jnp.broadcast_to(block[None], (lax.axis_size(axis),) + block.shape)
    return lax.all_to_all(copies, axis, split_axis=0, concat_axis=0, tiled=True)


def gather_rows(block):
    q, columns = block.shape
    nx, nz, nc = (lax.axis_size(a) for a in ROWS)
    along_z = gather_axis(block, "z")
    along_x = gather_axis(along_z, "x")
    mine = along_x.reshape(nx * nz, q, columns)
    other = lax.ppermute(mine, "core", [(i, (i + 1) % nc) for i in range(nc)])
    first = lax.axis_index("core") == 0
    both = jnp.stack([jnp.where(first, mine, other), jnp.where(first, other, mine)], axis=1)
    return both.reshape(nx * nz * nc * q, columns)


def redistribute(targets, send_order, send_count, recv_slot):
    groups = lax.axis_size(ROWS)
    arrived = lax.all_to_all(targets, "rhs", split_axis=1, concat_axis=0, tiled=True)
    rows_local, columns = arrived.shape
    capacity = 4
    counts = send_count[0]
    dest = jnp.arange(groups, dtype=jnp.int32)
    starts = jnp.sum(jnp.where(dest[None, :] < dest[:, None], counts[None, :], 0), axis=1)
    slot_number = jnp.arange(capacity, dtype=jnp.int32)
    listed = starts[:, None] + slot_number[None, :]
    filled = slot_number[None, :] < counts[:, None]
    index = jnp.arange(rows_local, dtype=jnp.int32)
    position = jnp.sum(jnp.where(send_order[:, None] == index[None, :], index[:, None], 0), axis=0)
    picks = (jnp.where(filled, listed, -1)[:, :, None] == position[None, None, :])
    picked = picks.reshape(groups * capacity, rows_local).astype(jnp.float32)
    outgoing = product(picked, arrived).reshape(groups, capacity, columns)
    labels = jnp.sum(jnp.where(picks, recv_slot[None, None, :], 0), axis=2)
    labels = jnp.where(filled, labels, rows_local).astype(jnp.float32)
    labels = jnp.broadcast_to(labels[:, :, None], (groups, capacity, columns // capacity))
    sent = jnp.concatenate([outgoing, labels.reshape(groups, 1, columns)], axis=1)
    incoming = lax.all_to_all(sent, ROWS, split_axis=0, concat_axis=0, tiled=True)
    landing = incoming[:, capacity].reshape(groups, capacity, columns // capacity)[:, :, 0]
    placed = landing.astype(jnp.int32)[:, :, None] == index[None, None, :]
    placed = placed.astype(jnp.float32).reshape(groups * capacity, rows_local)
    rows = incoming[:, :capacity].reshape(groups * capacity, columns)
    return lax.dot_general(
        placed,
        rows,
        (((0,), (0,)), ((), ())),
        precision=lax.Precision.HIGHEST,
        preferred_element_type=jnp.float32,
    )


def shards(targets, send_order, send_count, recv_slot, panel, inv_diag):
    sections, block_rows, share_rows = inv_diag.shape
    inverse_rows = lax.all_to_all(inv_diag, ROWS, split_axis=1, concat_axis=2, tiled=True)
    residual = redistribute(targets, send_order, send_count, recv_slot)
    square = sections * share_rows
    top = residual[:square]
    below = residual[square:]
    finished = []
    for k in range(sections):
        pending = gather_rows(top[:share_rows])
        owned = product(inverse_rows[k], pending)
        finished.append(owned)
        solved = gather_rows(owned)
        columns_block = panel[:, k * block_rows : (k + 1) * block_rows]
        if k + 1 < sections:
            top = top[share_rows:] - product(
                columns_block[(k + 1) * share_rows : square], solved
            )
        below = below - product(columns_block[square:], solved)
    return jnp.concatenate(finished + [below], axis=0)


def solution(mesh):
    ny = mesh.shape["rhs"]
    split = Mesh(mesh.devices.reshape(4, 16, 2, ny), ROWS + ("rhs",))
    placed = (
        P(ROWS + ("rhs",), None),
        P(ROWS),
        P(ROWS, None),
        P(ROWS),
        P(ROWS, None),
        P(None, None, ROWS),
    )
    return jax.shard_map(
        shards, mesh=split, in_specs=placed, out_specs=P(ROWS, "rhs"), check_vma=False
    )
```

```python
import jax
import jax.numpy as jnp
from jax import lax
from jax.sharding import Mesh, PartitionSpec as P

ROWS = ("x", "z", "core")
SWAP = [(0, 1), (1, 0)]


def product(left, right, contract=((1,), (0,))):
    return lax.dot_general(
        left,
        right,
        (contract, ((), ())),
        precision=lax.Precision.HIGHEST,
        preferred_element_type=jnp.float32,
    )


def redistribute(targets, send_order, send_count, recv_slot):
    groups = lax.axis_size(ROWS)
    arrived = lax.all_to_all(targets, "rhs", split_axis=1, concat_axis=0, tiled=True)
    rows_local, columns = arrived.shape
    capacity, tag = 4, 128
    counts = send_count[0]
    dest = jnp.arange(groups, dtype=jnp.int32)
    starts = jnp.sum(jnp.where(dest[None, :] < dest[:, None], counts[None, :], 0), axis=1)
    slot_number = jnp.arange(capacity, dtype=jnp.int32)
    listed = starts[:, None] + slot_number[None, :]
    listed = jnp.where(slot_number[None, :] < counts[:, None], listed, -1)
    index = jnp.arange(rows_local, dtype=jnp.int32)
    position = jnp.sum(jnp.where(send_order[:, None] == index[None, :], index[:, None], 0), axis=0)
    picked = (listed[:, :, None] == position[None, None, :]).astype(jnp.float32)
    picked = picked.reshape(groups * capacity, rows_local)
    landing = jnp.broadcast_to((recv_slot + 1).astype(jnp.float32)[:, None], (rows_local, tag))
    sent = product(picked, jnp.concatenate([arrived, landing], axis=1))
    incoming = lax.all_to_all(
        sent.reshape(groups, capacity, columns + tag), ROWS, split_axis=0, concat_axis=0, tiled=True
    ).reshape(groups * capacity, columns + tag)
    slots = (incoming[:, columns : columns + 1] - 1.0).astype(jnp.int32)
    placed = (slots == index[None, :]).astype(jnp.float32)
    return product(placed, incoming[:, :columns], ((0,), (0,)))


def shards(targets, send_order, send_count, recv_slot, panel, inv_diag):
    sections, block_rows, share = inv_diag.shape
    nx, nz, nc = (lax.axis_size(a) for a in ROWS)
    first = lax.axis_index("core") == 0
    square = sections * share
    pairs = [(j, k) for j in range(1, sections) for k in range(j)]
    tiles = [
        panel[j * share : (j + 1) * share, k * block_rows : (k + 1) * block_rows] for j, k in pairs
    ]
    local = jnp.concatenate([jnp.stack(tiles), jnp.swapaxes(inv_diag, 1, 2)], axis=0)
    weights = lax.all_gather(local, "z")

    def weight(i):
        return weights[:, i].reshape(nz * share, block_rows)

    residual = redistribute(targets, send_order, send_count, recv_slot)
    columns = residual.shape[1]
    tops = lax.all_gather(residual[:square].reshape(sections, share, columns), "z")
    pending = [tops[:, k].reshape(nz * share, columns) for k in range(sections)]
    below = residual[square:]
    finished = []
    for k in range(sections):
        partial = product(weight(len(pairs) + k), pending[k], ((0,), (0,)))
        partial = partial.reshape(nx * nz, nc, share, columns)
        keep = jnp.where(first, partial[:, 0], partial[:, 1])
        give = jnp.where(first, partial[:, 1], partial[:, 0])
        half = keep + lax.ppermute(give, "core", SWAP)
        half = half.reshape(nx, nz, share, columns)
        owned = jnp.sum(
            lax.all_to_all(half, "x", split_axis=0, concat_axis=0, tiled=True), axis=0
        )
        finished.append(lax.dynamic_index_in_dim(owned, lax.axis_index("z"), 0, keepdims=False))
        copies = jnp.broadcast_to(owned[None], (nx,) + owned.shape)
        mine = lax.all_to_all(copies, "x", split_axis=0, concat_axis=0, tiled=True)
        mine = mine.reshape(nx * nz, share, columns)
        other = lax.ppermute(mine, "core", SWAP)
        solved = jnp.stack([jnp.where(first, mine, other), jnp.where(first, other, mine)], axis=1)
        solved = solved.reshape(block_rows, columns)
        for j in range(k + 1, sections):
            pending[j] = pending[j] - product(weight(pairs.index((j, k))), solved)
        below = below - product(panel[square:, k * block_rows : (k + 1) * block_rows], solved)
    return jnp.concatenate(finished + [below], axis=0)


def solution(mesh):
    ny = mesh.shape["rhs"]
    split = Mesh(mesh.devices.reshape(4, 16, 2, ny), ROWS + ("rhs",))
    placed = (
        P(ROWS + ("rhs",), None),
        P(ROWS),
        P(ROWS, None),
        P(ROWS),
        P(ROWS, None),
        P(None, None, ROWS),
    )
    return jax.shard_map(
        shards, mesh=split, in_specs=placed, out_specs=P(ROWS, "rhs"), check_vma=False
    )
```

```python
import jax
import jax.numpy as jnp
from jax import lax
from jax.sharding import Mesh, PartitionSpec as P

ROWS = ("x", "z", "core")
SWAP = [(0, 1), (1, 0)]


def product(left, right, contract=((1,), (0,))):
    return lax.dot_general(
        left,
        right,
        (contract, ((), ())),
        precision=lax.Precision.HIGHEST,
        preferred_element_type=jnp.float32,
    )


def redistribute(targets, send_order, send_count, recv_slot):
    groups = lax.axis_size(ROWS)
    arrived = lax.all_to_all(targets, "rhs", split_axis=1, concat_axis=0, tiled=True)
    rows_local, columns = arrived.shape
    capacity, tag = 4, 64
    counts = send_count[0]
    dest = jnp.arange(groups, dtype=jnp.int32)
    starts = jnp.sum(jnp.where(dest[None, :] < dest[:, None], counts[None, :], 0), axis=1)
    index = jnp.arange(rows_local, dtype=jnp.int32)
    position = jnp.sum(jnp.where(send_order[:, None] == index[None, :], index[:, None], 0), axis=0)
    slot_number = jnp.arange(capacity, dtype=jnp.int32)
    listed = starts[None, :] + slot_number[:, None]
    listed = jnp.where(slot_number[:, None] < counts[None, :], listed, -1)
    picked = (listed[:, :, None] == position[None, None, :]).astype(jnp.float32)
    picked = picked.reshape(capacity * groups, rows_local)
    landing = jnp.broadcast_to((recv_slot + 1).astype(jnp.float32)[:, None], (rows_local, 2 * tag))
    planes = product(picked, jnp.concatenate([arrived, landing], axis=1))
    planes = planes.reshape(capacity, groups, columns + 2 * tag)
    halves = [
        jnp.concatenate(
            [
                planes[s, :, :columns],
                planes[s + 1, :, :columns],
                planes[s, :, columns : columns + tag],
                planes[s + 1, :, columns : columns + tag],
            ],
            axis=1,
        )
        for s in range(0, capacity, 2)
    ]
    incoming = lax.all_to_all(
        jnp.stack(halves, axis=1), ROWS, split_axis=0, concat_axis=0, tiled=True
    )
    total = 0.0
    for h in range(capacity // 2):
        half = incoming[:, h]
        for s in range(2):
            label = half[:, 2 * columns + s * tag : 2 * columns + s * tag + 1] - 1.0
            placed = (label.astype(jnp.int32) == index[None, :]).astype(jnp.float32)
            rows = half[:, s * columns : (s + 1) * columns]
            total = total + product(placed, rows, ((0,), (0,)))
    return total


def shards(targets, send_order, send_count, recv_slot, panel, inv_diag):
    sections, block_rows, share = inv_diag.shape
    nx, nz, nc = (lax.axis_size(a) for a in ROWS)
    zi = lax.axis_index("z")
    first = lax.axis_index("core") == 0
    even = zi % 2 == 0
    square = sections * share
    inverse_columns = jnp.swapaxes(inv_diag, 1, 2)

    def tile(j, k):
        if j == k:
            return inverse_columns[k]
        return panel[j * share : (j + 1) * share, k * block_rows : (k + 1) * block_rows]

    weight = {}
    early = [(0, 0), (1, 0)]
    late = [(j, k) for j in range(sections) for k in range(j + 1) if (j, k) not in early]
    for names in (early, late):
        gathered = lax.all_gather(jnp.stack([tile(j, k) for j, k in names]), "z")
        for i, name in enumerate(names):
            weight[name] = gathered[:, i].reshape(nz * share, block_rows)

    residual = redistribute(targets, send_order, send_count, recv_slot)
    columns = residual.shape[1] // 2
    halves = jnp.stack([residual[:square, :columns], residual[:square, columns:]])
    tops = jnp.broadcast_to(halves[None], (nz // 2,) + halves.shape).reshape(nz, square, columns)
    tops = lax.all_to_all(tops, "z", split_axis=0, concat_axis=0, tiled=True)
    pending = [
        tops[:, k * share : (k + 1) * share].reshape(nz * share, columns) for k in range(sections)
    ]
    left, right = residual[square:, :columns], residual[square:, columns:]
    below = [jnp.where(even, left, right), jnp.where(even, right, left)]
    start = ((lax.axis_index("x") * nz + zi) * nc + lax.axis_index("core")) * share
    finished = []
    for k in range(sections):
        partial = product(weight[(k, k)], pending[k], ((0,), (0,)))
        partial = partial.reshape(nx * nz, nc, share, columns)
        keep = jnp.where(first, partial[:, 0], partial[:, 1])
        give = jnp.where(first, partial[:, 1], partial[:, 0])
        half = keep + lax.ppermute(give, "core", SWAP)
        copies = jnp.broadcast_to(half[None], (nx,) + half.shape)
        mine = jnp.sum(lax.all_to_all(copies, "x", split_axis=0, concat_axis=0, tiled=True), axis=0)
        other = lax.ppermute(mine, "core", SWAP)
        solved = jnp.stack([jnp.where(first, mine, other), jnp.where(first, other, mine)], axis=1)
        solved = solved.reshape(block_rows, columns)
        for j in range(k + 1, sections):
            pending[j] = pending[j] - product(weight[(j, k)], solved)
        traded = lax.ppermute(solved, "z", [(i, i ^ 1) for i in range(nz)])
        factor = panel[square:, k * block_rows : (k + 1) * block_rows]
        pieces = []
        for h, block in enumerate((solved, traded)):
            below[h] = below[h] - product(factor, block)
            pieces.append(lax.dynamic_slice_in_dim(block, start, share, 0))
        finished.append(pieces)
    ends = [jnp.concatenate([f[h] for f in finished] + [below[h]], axis=0) for h in range(2)]
    return jnp.concatenate(
        [jnp.where(even, ends[0], ends[1]), jnp.where(even, ends[1], ends[0])], axis=1
    )


def solution(mesh):
    ny = mesh.shape["rhs"]
    split = Mesh(mesh.devices.reshape(4, 16, 2, ny), ROWS + ("rhs",))
    placed = (
        P(ROWS + ("rhs",), None),
        P(ROWS),
        P(ROWS, None),
        P(ROWS),
        P(ROWS, None),
        P(None, None, ROWS),
    )
    return jax.shard_map(
        shards, mesh=split, in_specs=placed, out_specs=P(ROWS, "rhs"), check_vma=False
    )
```

```python
import jax
import jax.numpy as jnp
from jax import lax
from jax.experimental import pallas as pl
from jax.experimental.pallas import tpu as pltpu
from jax.sharding import Mesh, PartitionSpec as P

ROWS = ("x", "z", "core")
SWAP = [(0, 1), (1, 0)]


def product(left, right, contract=((1,), (0,)), precision=lax.Precision.HIGHEST):
    return lax.dot_general(
        left,
        right,
        (contract, ((), ())),
        precision=precision,
        preferred_element_type=jnp.float32,
    )


def quick(left, right, contract=((1,), (0,))):
    return product(left, right, contract, lax.Precision.HIGH)


def pack_tiles(panel, inverse_columns, names):
    sections, share, width = inverse_columns.shape

    def kernel(panel_ref, inverse_ref, out_ref, sems):
        copies = []
        for i, (j, k) in enumerate(names):
            if j == k:
                source = inverse_ref.at[k]
            else:
                source = panel_ref.at[pl.ds(j * share, share), pl.ds(k * width, width)]
            copies.append(pltpu.make_async_copy(source, out_ref.at[i], sems.at[i]))
        for copy in copies:
            copy.start()
        for copy in copies:
            copy.wait()

    anywhere = pl.BlockSpec(memory_space=pltpu.HBM)
    return pl.pallas_call(
        kernel,
        out_shape=jax.ShapeDtypeStruct((len(names), share, width), jnp.float32),
        in_specs=[anywhere, anywhere],
        out_specs=anywhere,
        scratch_shapes=[pltpu.SemaphoreType.DMA((len(names),))],
    )(panel, inverse_columns)


def redistribute(targets, send_order, send_count, recv_slot, beside):
    groups = lax.axis_size(ROWS)
    arrived = lax.all_to_all(targets, "rhs", split_axis=1, concat_axis=0, tiled=True)
    rows_local, columns = arrived.shape
    capacity, tag = 4, 64
    counts = send_count[0]
    dest = jnp.arange(groups, dtype=jnp.int32)
    starts = jnp.sum(jnp.where(dest[None, :] < dest[:, None], counts[None, :], 0), axis=1)
    index = jnp.arange(rows_local, dtype=jnp.int32)
    position = jnp.sum(jnp.where(send_order[:, None] == index[None, :], index[:, None], 0), axis=0)
    slot_number = jnp.arange(capacity, dtype=jnp.int32)
    listed = starts[None, :] + slot_number[:, None]
    listed = jnp.where(slot_number[:, None] < counts[None, :], listed, -1)
    picked = (listed[:, :, None] == position[None, None, :]).astype(jnp.float32)
    picked = picked.reshape(capacity * groups, rows_local)
    landing = jnp.broadcast_to((recv_slot + 1).astype(jnp.float32)[:, None], (rows_local, 2 * tag))
    planes = product(picked, jnp.concatenate([arrived, landing], axis=1))
    planes = planes.reshape(capacity, groups, columns + 2 * tag)
    halves = [
        jnp.concatenate(
            [
                planes[s, :, :columns],
                planes[s + 1, :, :columns],
                planes[s, :, columns : columns + tag],
                planes[s + 1, :, columns : columns + tag],
            ],
            axis=1,
        )
        for s in range(0, capacity, 2)
    ]
    sent, beside = lax.optimization_barrier((jnp.stack(halves, axis=1), beside))
    gathered = lax.all_gather(beside, "z")
    incoming = lax.all_to_all(
        sent, ROWS, split_axis=0, concat_axis=0, tiled=True
    )
    incoming, gathered = lax.optimization_barrier((incoming, gathered))
    total = 0.0
    for h in range(capacity // 2):
        half = incoming[:, h]
        for s in range(2):
            label = half[:, 2 * columns + s * tag : 2 * columns + s * tag + 1] - 1.0
            placed = (label.astype(jnp.int32) == index[None, :]).astype(jnp.float32)
            rows = half[:, s * columns : (s + 1) * columns]
            total = total + product(placed, rows, ((0,), (0,)))
    return total, gathered


def whole_block(mine, first):
    other = lax.ppermute(mine, "core", SWAP)
    both = jnp.stack([jnp.where(first, mine, other), jnp.where(first, other, mine)], axis=1)
    return both.reshape(2 * mine.shape[0] * mine.shape[1], mine.shape[2])


def shards(targets, send_order, send_count, recv_slot, panel, inv_diag):
    sections, block_rows, share = inv_diag.shape
    nx, nz, nc = (lax.axis_size(a) for a in ROWS)
    zi = lax.axis_index("z")
    first = lax.axis_index("core") == 0
    even = zi % 2 == 0
    square = sections * share
    inverse_columns = jnp.swapaxes(inv_diag, 1, 2)

    weight = {}
    names = [(j, k) for j in range(sections) for k in range(j + 1)][1:]
    gathered = lax.all_gather(pack_tiles(panel, inverse_columns, names), "z")
    for i, name in enumerate(names):
        weight[name] = gathered[:, i].reshape(nz * share, block_rows)
    residual, lead = redistribute(
        targets, send_order, send_count, recv_slot, inverse_columns[0]
    )
    weight[(0, 0)] = lead.reshape(nz * share, block_rows)
    columns = residual.shape[1] // 2
    halves = jnp.stack([residual[:square, :columns], residual[:square, columns:]])
    tops = jnp.broadcast_to(halves[None], (nz // 2,) + halves.shape).reshape(nz, square, columns)
    tops = lax.all_to_all(tops, "z", split_axis=0, concat_axis=0, tiled=True)
    pending = [
        tops[:, k * share : (k + 1) * share].reshape(nz * share, columns) for k in range(sections)
    ]
    left, right = residual[square:, :columns], residual[square:, columns:]
    below = [jnp.where(even, left, right), jnp.where(even, right, left)]
    start = ((lax.axis_index("x") * nz + zi) * nc + lax.axis_index("core")) * share
    finished = []
    for k in range(sections):
        partial = quick(weight[(k, k)], pending[k], ((0,), (0,)))
        partial = partial.reshape(nx * nz, nc, share, columns)
        keep = jnp.where(first, partial[:, 0], partial[:, 1])
        give = jnp.where(first, partial[:, 1], partial[:, 0])
        half = keep + lax.ppermute(give, "core", SWAP)
        copies = jnp.broadcast_to(half[None], (nx,) + half.shape)
        mine = jnp.sum(lax.all_to_all(copies, "x", split_axis=0, concat_axis=0, tiled=True), axis=0)
        solved = whole_block(mine, first)
        for j in range(k + 1, sections):
            pending[j] = pending[j] - quick(weight[(j, k)], solved)
        traded = whole_block(lax.ppermute(mine, "z", [(i, i ^ 1) for i in range(nz)]), first)
        factor = panel[square:, k * block_rows : (k + 1) * block_rows]
        pieces = []
        for h, block in enumerate((solved, traded)):
            below[h] = below[h] - quick(factor, block)
            pieces.append(lax.dynamic_slice_in_dim(block, start, share, 0))
        finished.append(pieces)
    ends = [jnp.concatenate([f[h] for f in finished] + [below[h]], axis=0) for h in range(2)]
    return jnp.concatenate(
        [jnp.where(even, ends[0], ends[1]), jnp.where(even, ends[1], ends[0])], axis=1
    )


def solution(mesh):
    ny = mesh.shape["rhs"]
    split = Mesh(mesh.devices.reshape(4, 16, 2, ny), ROWS + ("rhs",))
    placed = (
        P(ROWS + ("rhs",), None),
        P(ROWS),
        P(ROWS, None),
        P(ROWS),
        P(ROWS, None),
        P(None, None, ROWS),
    )
    return jax.shard_map(
        shards, mesh=split, in_specs=placed, out_specs=P(ROWS, "rhs"), check_vma=False
    )
```

```python
import jax
import jax.numpy as jnp
from jax import lax
from jax.sharding import Mesh, PartitionSpec as P

ROWS = ("x", "z", "core")
SWAP = [(0, 1), (1, 0)]


def product(left, right, contract=((1,), (0,))):
    return lax.dot_general(
        left,
        right,
        (contract, ((), ())),
        precision=lax.Precision.HIGHEST,
        preferred_element_type=jnp.float32,
    )


def ring(block, steps, hop, size, axis):
    held = []
    for _ in range(steps):
        block = lax.ppermute(block, axis, [(i, (i + hop) % size) for i in range(size)])
        held.append(block)
    return held


def redistribute(targets, send_order, send_count, recv_slot, tips):
    groups = lax.axis_size(ROWS)
    arrived = lax.all_to_all(targets, "rhs", split_axis=1, concat_axis=0, tiled=True)
    rows_local, columns = arrived.shape
    capacity, tag = 4, 64
    counts = send_count[0]
    dest = jnp.arange(groups, dtype=jnp.int32)
    starts = jnp.sum(jnp.where(dest[None, :] < dest[:, None], counts[None, :], 0), axis=1)
    index = jnp.arange(rows_local, dtype=jnp.int32)
    position = jnp.sum(jnp.where(send_order[:, None] == index[None, :], index[:, None], 0), axis=0)
    slot_number = jnp.arange(capacity, dtype=jnp.int32)
    listed = starts[None, :] + slot_number[:, None]
    listed = jnp.where(slot_number[:, None] < counts[None, :], listed, -1)
    picked = (listed[:, :, None] == position[None, None, :]).astype(jnp.float32)
    picked = picked.reshape(capacity * groups, rows_local)
    landing = jnp.broadcast_to((recv_slot + 1).astype(jnp.float32)[:, None], (rows_local, 2 * tag))
    planes = product(picked, jnp.concatenate([arrived, landing], axis=1))
    planes = planes.reshape(capacity, groups, columns + 2 * tag)
    halves = [
        jnp.concatenate(
            [
                planes[s, :, :columns],
                planes[s + 1, :, :columns],
                planes[s, :, columns : columns + tag],
                planes[s + 1, :, columns : columns + tag],
            ],
            axis=1,
        )
        for s in range(0, capacity, 2)
    ]
    incoming = lax.all_to_all(
        jnp.stack(halves, axis=1), ROWS, split_axis=0, concat_axis=0, tiled=True
    )
    incoming, tips = lax.optimization_barrier((incoming, tips))
    total = 0.0
    for h in range(capacity // 2):
        half = incoming[:, h]
        for s in range(2):
            label = half[:, 2 * columns + s * tag : 2 * columns + s * tag + 1] - 1.0
            placed = (label.astype(jnp.int32) == index[None, :]).astype(jnp.float32)
            rows = half[:, s * columns : (s + 1) * columns]
            total = total + product(placed, rows, ((0,), (0,)))
    return total, tips


def whole_block(mine, first):
    other = lax.ppermute(mine, "core", SWAP)
    both = jnp.stack([jnp.where(first, mine, other), jnp.where(first, other, mine)], axis=1)
    return both.reshape(2 * mine.shape[0] * mine.shape[1], mine.shape[2])


def shards(targets, send_order, send_count, recv_slot, panel, inv_diag):
    sections, block_rows, share = inv_diag.shape
    nx, nz, nc = (lax.axis_size(a) for a in ROWS)
    zi = lax.axis_index("z")
    first = lax.axis_index("core") == 0
    even = zi % 2 == 0
    square = sections * share
    inverse_columns = jnp.swapaxes(inv_diag, 1, 2)

    names = [(j, k) for j in range(sections) for k in range(j + 1)]
    own = jnp.stack(
        [
            inverse_columns[k]
            if j == k
            else panel[j * share : (j + 1) * share, k * block_rows : (k + 1) * block_rows]
            for j, k in names
        ]
    )
    up, down = ring(own, 5, 1, nz, "z"), ring(own, 5, -1, nz, "z")
    residual, (up[-1], down[-1]) = redistribute(
        targets, send_order, send_count, recv_slot, (up[-1], down[-1])
    )
    up += ring(up[-1], nz // 2 - 5, 1, nz, "z")
    down += ring(down[-1], nz // 2 - 6, -1, nz, "z")
    around = [own] + down + up[::-1]
    weight = {
        name: jnp.concatenate([chunk[i] for chunk in around], axis=0)
        for i, name in enumerate(names)
    }
    columns = residual.shape[1] // 2
    halves = jnp.stack([residual[:square, :columns], residual[:square, columns:]])
    tops = jnp.broadcast_to(halves[None], (nz // 2,) + halves.shape).reshape(nz, square, columns)
    tops = lax.all_to_all(tops, "z", split_axis=0, concat_axis=0, tiled=True)
    tops = lax.dynamic_slice_in_dim(jnp.concatenate([tops, tops[:-1]], axis=0), zi, nz, 0)
    pending = [
        tops[:, k * share : (k + 1) * share].reshape(nz * share, columns) for k in range(sections)
    ]
    left, right = residual[square:, :columns], residual[square:, columns:]
    below = [jnp.where(even, left, right), jnp.where(even, right, left)]
    start = ((lax.axis_index("x") * nz + zi) * nc + lax.axis_index("core")) * share
    finished = []
    for k in range(sections):
        partial = product(weight[(k, k)], pending[k], ((0,), (0,)))
        partial = partial.reshape(nx * nz, nc, share, columns)
        keep = jnp.where(first, partial[:, 0], partial[:, 1])
        give = jnp.where(first, partial[:, 1], partial[:, 0])
        half = keep + lax.ppermute(give, "core", SWAP)
        copies = jnp.broadcast_to(half[None], (nx,) + half.shape)
        mine = jnp.sum(lax.all_to_all(copies, "x", split_axis=0, concat_axis=0, tiled=True), axis=0)
        solved = whole_block(mine, first)
        for j in range(k + 1, sections):
            pending[j] = pending[j] - product(weight[(j, k)], solved)
        traded = whole_block(lax.ppermute(mine, "z", [(i, i ^ 1) for i in range(nz)]), first)
        factor = panel[square:, k * block_rows : (k + 1) * block_rows]
        pieces = []
        for h, block in enumerate((solved, traded)):
            below[h] = below[h] - product(factor, block)
            pieces.append(lax.dynamic_slice_in_dim(block, start, share, 0))
        finished.append(pieces)
    ends = [jnp.concatenate([f[h] for f in finished] + [below[h]], axis=0) for h in range(2)]
    return jnp.concatenate(
        [jnp.where(even, ends[0], ends[1]), jnp.where(even, ends[1], ends[0])], axis=1
    )


def solution(mesh):
    ny = mesh.shape["rhs"]
    split = Mesh(mesh.devices.reshape(4, 16, 2, ny), ROWS + ("rhs",))
    placed = (
        P(ROWS + ("rhs",), None),
        P(ROWS),
        P(ROWS, None),
        P(ROWS),
        P(ROWS, None),
        P(None, None, ROWS),
    )
    return jax.shard_map(
        shards, mesh=split, in_specs=placed, out_specs=P(ROWS, "rhs"), check_vma=False
    )
```

```python
import jax
import jax.numpy as jnp
from jax import lax
from jax.sharding import Mesh, PartitionSpec as P

ROWS = ("x", "z", "core")
SWAP = [(0, 1), (1, 0)]


def product(left, right, contract=((1,), (0,))):
    return lax.dot_general(
        left,
        right,
        (contract, ((), ())),
        precision=lax.Precision.HIGHEST,
        preferred_element_type=jnp.float32,
    )


def shift(block, axis, hop):
    n = lax.axis_size(axis)
    return lax.ppermute(block, axis, [(i, (i - hop) % n) for i in range(n)])


def around(block):
    near = jnp.stack([block] + [shift(block, "x", hop) for hop in range(1, lax.axis_size("x"))])
    return jnp.stack([near, lax.ppermute(near, "core", SWAP)])


def redistribute(targets, send_order, send_count, recv_slot):
    groups = lax.axis_size(ROWS)
    arrived = lax.all_to_all(targets, "rhs", split_axis=1, concat_axis=0, tiled=True)
    rows_local, columns = arrived.shape
    capacity, tag = 4, 64
    counts = send_count[0]
    dest = jnp.arange(groups, dtype=jnp.int32)
    starts = jnp.sum(jnp.where(dest[None, :] < dest[:, None], counts[None, :], 0), axis=1)
    index = jnp.arange(rows_local, dtype=jnp.int32)
    position = jnp.sum(jnp.where(send_order[:, None] == index[None, :], index[:, None], 0), axis=0)
    slot_number = jnp.arange(capacity, dtype=jnp.int32)
    listed = starts[None, :] + slot_number[:, None]
    listed = jnp.where(slot_number[:, None] < counts[None, :], listed, -1)
    picked = (listed[:, :, None] == position[None, None, :]).astype(jnp.float32)
    picked = picked.reshape(capacity * groups, rows_local)
    landing = jnp.broadcast_to((recv_slot + 1).astype(jnp.float32)[:, None], (rows_local, 2 * tag))
    planes = product(picked, jnp.concatenate([arrived, landing], axis=1))
    planes = planes.reshape(capacity, groups, columns + 2 * tag)
    halves = [
        jnp.concatenate(
            [
                planes[s, :, :columns],
                planes[s + 1, :, :columns],
                planes[s, :, columns : columns + tag],
                planes[s + 1, :, columns : columns + tag],
            ],
            axis=1,
        )
        for s in range(0, capacity, 2)
    ]
    incoming = lax.all_to_all(
        jnp.stack(halves, axis=1), ROWS, split_axis=0, concat_axis=0, tiled=True
    )
    total = 0.0
    for h in range(capacity // 2):
        half = incoming[:, h]
        for s in range(2):
            label = half[:, 2 * columns + s * tag : 2 * columns + s * tag + 1] - 1.0
            placed = (label.astype(jnp.int32) == index[None, :]).astype(jnp.float32)
            rows = half[:, s * columns : (s + 1) * columns]
            total = total + product(placed, rows, ((0,), (0,)))
    return total


def shards(targets, send_order, send_count, recv_slot, panel, inv_diag):
    sections, width, share = inv_diag.shape
    nx, nz, nc = (lax.axis_size(a) for a in ROWS)
    xi, zi, ci = (lax.axis_index(a) for a in ROWS)
    first = ci == 0
    square = sections * share
    part = nx * nc * share

    lane = jnp.arange(width, dtype=jnp.int32)
    inner = nc * share
    moved = (lane // inner % nz) * part + lane // (nz * inner) * inner + lane % inner
    order = (moved[:, None] == lane[None, :]).astype(jnp.float32)

    names = [(j, k) for j in range(sections) for k in range(j + 1)]
    inverse_columns = jnp.swapaxes(inv_diag, 1, 2)
    own = jnp.concatenate(
        [
            inverse_columns[k]
            if j == k
            else panel[j * share : (j + 1) * share, k * width : (k + 1) * width]
            for j, k in names
        ],
        axis=0,
    )
    own = product(own, order).reshape(len(names), share, width)
    gathered = around(own)
    weight = {name: gathered[:, :, i].reshape(part, width) for i, name in enumerate(names)}

    residual = redistribute(targets, send_order, send_count, recv_slot)
    rows, columns = residual.shape
    slim = columns // (nx * nc)
    tops = residual[:square].reshape(square, nx * nc, slim).transpose(1, 0, 2)
    tops = lax.all_to_all(tops, ("x", "core"), split_axis=0, concat_axis=0, tiled=True)
    tops = tops.reshape(nx, nc, square, slim)
    tops = lax.dynamic_slice_in_dim(jnp.concatenate([tops, tops[:-1]], axis=0), xi, nx, 0)
    tops = jnp.stack(
        [
            jnp.where(first, tops[:, 0], tops[:, 1]),
            jnp.where(first, tops[:, 1], tops[:, 0]),
        ]
    )
    pending = [
        tops[:, :, k * share : (k + 1) * share].reshape(part, slim) for k in range(sections)
    ]

    mine = zi * part + xi * inner + ci * share + jnp.arange(share, dtype=jnp.int32)
    pick = (mine[:, None] == lane[None, :]).astype(jnp.float32)
    below = residual[square:]
    finished = []
    half = slim // 2
    for k in range(sections):
        fold = jnp.concatenate(
            [
                product(pending[k][:, h : h + half], weight[(k, k)], ((0,), (0,))).reshape(
                    half, nz, part
                )
                for h in (0, half)
            ],
            axis=2,
        ).transpose(1, 0, 2)
        fold = lax.all_to_all(fold, "z", split_axis=0, concat_axis=0, tiled=True)
        fold = jnp.broadcast_to(jnp.sum(fold, axis=0)[None], fold.shape)
        fold = lax.all_to_all(fold, "z", split_axis=0, concat_axis=0, tiled=True)
        solved = jnp.concatenate(
            [fold[:, :, i * part : (i + 1) * part].transpose(1, 0, 2) for i in range(2)], axis=0
        ).reshape(slim, width)
        for j in range(k + 1, sections):
            pending[j] = pending[j] - product(weight[(j, k)], solved, ((1,), (1,)))
        every = around(solved)
        every = jnp.stack(
            [jnp.where(first, every[0], every[1]), jnp.where(first, every[1], every[0])], axis=1
        )
        every = jnp.concatenate([every, every[:-1]], axis=0)
        every = lax.dynamic_slice_in_dim(every, (nx - xi) % nx, nx, 0).reshape(columns, width)
        factor = product(panel[square:, k * width : (k + 1) * width], order)
        found = product(jnp.concatenate([pick, factor], axis=0), every, ((1,), (1,)))
        finished.append(found[:share])
        below = below - found[share:]
    return jnp.concatenate(finished + [below], axis=0)


def solution(mesh):
    ny = mesh.shape["rhs"]
    split = Mesh(mesh.devices.reshape(4, 16, 2, ny), ROWS + ("rhs",))
    placed = (
        P(ROWS + ("rhs",), None),
        P(ROWS),
        P(ROWS, None),
        P(ROWS),
        P(ROWS, None),
        P(None, None, ROWS),
    )
    return jax.shard_map(
        shards, mesh=split, in_specs=placed, out_specs=P(ROWS, "rhs"), check_vma=False
    )
```

```python
import jax
import jax.numpy as jnp
from jax import lax
from jax.experimental import pallas as pl
from jax.sharding import Mesh, PartitionSpec as P

ROWS = ("x", "z", "core")
SWAP = [(0, 1), (1, 0)]


def product(left, right, contract=((1,), (0,))):
    return lax.dot_general(
        left,
        right,
        (contract, ((), ())),
        precision=lax.Precision.HIGHEST,
        preferred_element_type=jnp.float32,
    )


def pack_tiles(panel, inverse_columns, batches):
    sections, share, width = inverse_columns.shape

    def kernel(panel_ref, inverse_ref, *out_refs):
        for out_ref, names in zip(out_refs, batches):
            for i, (j, k) in enumerate(names):
                if j == k:
                    out_ref[i] = inverse_ref[k]
                else:
                    out_ref[i] = panel_ref[j * share : (j + 1) * share, k * width : (k + 1) * width]

    return pl.pallas_call(
        kernel,
        grid=(1,),
        out_shape=[jax.ShapeDtypeStruct((len(b), share, width), jnp.float32) for b in batches],
        in_specs=[
            pl.BlockSpec((sections * share, (sections - 1) * width), lambda i: (0, 0)),
            pl.BlockSpec((sections, share, width), lambda i: (0, 0, 0)),
        ],
        out_specs=[pl.BlockSpec((len(b), share, width), lambda i: (0, 0, 0)) for b in batches],
    )(panel, inverse_columns)


def redistribute(targets, send_order, send_count, recv_slot):
    groups = lax.axis_size(ROWS)
    arrived = lax.all_to_all(targets, "rhs", split_axis=1, concat_axis=0, tiled=True)
    rows_local, columns = arrived.shape
    capacity, tag = 4, 64
    counts = send_count[0]
    dest = jnp.arange(groups, dtype=jnp.int32)
    starts = jnp.sum(jnp.where(dest[None, :] < dest[:, None], counts[None, :], 0), axis=1)
    index = jnp.arange(rows_local, dtype=jnp.int32)
    position = jnp.sum(jnp.where(send_order[:, None] == index[None, :], index[:, None], 0), axis=0)
    slot_number = jnp.arange(capacity, dtype=jnp.int32)
    listed = starts[None, :] + slot_number[:, None]
    listed = jnp.where(slot_number[:, None] < counts[None, :], listed, -1)
    picked = (listed[:, :, None] == position[None, None, :]).astype(jnp.float32)
    picked = picked.reshape(capacity * groups, rows_local)
    landing = jnp.broadcast_to((recv_slot + 1).astype(jnp.float32)[:, None], (rows_local, 2 * tag))
    planes = product(picked, jnp.concatenate([arrived, landing], axis=1))
    planes = planes.reshape(capacity, groups, columns + 2 * tag)
    halves = [
        jnp.concatenate(
            [
                planes[s, :, :columns],
                planes[s + 1, :, :columns],
                planes[s, :, columns : columns + tag],
                planes[s + 1, :, columns : columns + tag],
            ],
            axis=1,
        )
        for s in range(0, capacity, 2)
    ]
    incoming = lax.all_to_all(
        jnp.stack(halves, axis=1), ROWS, split_axis=0, concat_axis=0, tiled=True
    )
    total = 0.0
    for h in range(capacity // 2):
        half = incoming[:, h]
        for s in range(2):
            label = half[:, 2 * columns + s * tag : 2 * columns + s * tag + 1] - 1.0
            placed = (label.astype(jnp.int32) == index[None, :]).astype(jnp.float32)
            rows = half[:, s * columns : (s + 1) * columns]
            total = total + product(placed, rows, ((0,), (0,)))
    return total


def whole_block(mine, first):
    other = lax.ppermute(mine, "core", SWAP)
    both = jnp.stack([jnp.where(first, mine, other), jnp.where(first, other, mine)], axis=1)
    return both.reshape(2 * mine.shape[0] * mine.shape[1], mine.shape[2])


def shards(targets, send_order, send_count, recv_slot, panel, inv_diag):
    sections, block_rows, share = inv_diag.shape
    nx, nz, nc = (lax.axis_size(a) for a in ROWS)
    zi = lax.axis_index("z")
    first = lax.axis_index("core") == 0
    even = zi % 2 == 0
    square = sections * share
    inverse_columns = jnp.swapaxes(inv_diag, 1, 2)

    weight = {}
    names = [(j, k) for j in range(sections) for k in range(j + 1)]
    batches = names[:6], names[6:]
    soon, late = (
        lax.all_gather(tiles, "z") for tiles in pack_tiles(panel, inverse_columns, batches)
    )
    for i, name in enumerate(names[:6]):
        weight[name] = soon[:, i].reshape(nz * share, block_rows)

    residual = redistribute(targets, send_order, send_count, recv_slot)
    columns = residual.shape[1] // 2
    halves = jnp.stack([residual[:square, :columns], residual[:square, columns:]])
    tops = jnp.broadcast_to(halves[None], (nz // 2,) + halves.shape).reshape(nz, square, columns)
    tops = lax.all_to_all(tops, "z", split_axis=0, concat_axis=0, tiled=True)
    pending = [
        tops[:, k * share : (k + 1) * share].reshape(nz * share, columns) for k in range(sections)
    ]
    left, right = residual[square:, :columns], residual[square:, columns:]
    below = [jnp.where(even, left, right), jnp.where(even, right, left)]
    start = ((lax.axis_index("x") * nz + zi) * nc + lax.axis_index("core")) * share
    finished, blocks = [], []
    for k in range(sections):
        partial = product(weight[(k, k)], pending[k], ((0,), (0,)))
        partial = partial.reshape(nx * nz, nc, share, columns)
        keep = jnp.where(first, partial[:, 0], partial[:, 1])
        give = jnp.where(first, partial[:, 1], partial[:, 0])
        half = keep + lax.ppermute(give, "core", SWAP)
        copies = jnp.broadcast_to(half[None], (nx,) + half.shape)
        mine = jnp.sum(lax.all_to_all(copies, "x", split_axis=0, concat_axis=0, tiled=True), axis=0)
        solved = whole_block(mine, first)
        blocks.append(solved)
        if k + 2 == sections:
            late = lax.optimization_barrier((mine, late))[1]
            for i, name in enumerate(names[6:]):
                weight[name] = late[:, i].reshape(nz * share, block_rows)
            for i, block in enumerate(blocks):
                pending[-1] = pending[-1] - product(weight[(sections - 1, i)], block)
        for j in range(k + 1, sections - 1):
            pending[j] = pending[j] - product(weight[(j, k)], solved)
        trade = [(i, i ^ 1) for i in range(nz)]
        if k + 1 < sections:
            traded = lax.ppermute(solved, "z", trade)
        else:
            traded = whole_block(lax.ppermute(mine, "z", trade), first)
        factor = panel[square:, k * block_rows : (k + 1) * block_rows]
        pieces = []
        for h, block in enumerate((solved, traded)):
            below[h] = below[h] - product(factor, block)
            pieces.append(lax.dynamic_slice_in_dim(block, start, share, 0))
        finished.append(pieces)
    ends = [jnp.concatenate([f[h] for f in finished] + [below[h]], axis=0) for h in range(2)]
    return jnp.concatenate(
        [jnp.where(even, ends[0], ends[1]), jnp.where(even, ends[1], ends[0])], axis=1
    )


def solution(mesh):
    ny = mesh.shape["rhs"]
    split = Mesh(mesh.devices.reshape(4, 16, 2, ny), ROWS + ("rhs",))
    placed = (
        P(ROWS + ("rhs",), None),
        P(ROWS),
        P(ROWS, None),
        P(ROWS),
        P(ROWS, None),
        P(None, None, ROWS),
    )
    return jax.shard_map(
        shards, mesh=split, in_specs=placed, out_specs=P(ROWS, "rhs"), check_vma=False
    )
```

```python
import jax
import jax.numpy as jnp
from jax import lax
from jax.experimental import pallas as pl
from jax.experimental.pallas import tpu as pltpu
from jax.sharding import Mesh, PartitionSpec as P

ROWS = ("x", "z", "core")
SWAP = [(0, 1), (1, 0)]


def product(left, right, contract=((1,), (0,))):
    return lax.dot_general(
        left,
        right,
        (contract, ((), ())),
        precision=lax.Precision.HIGHEST,
        preferred_element_type=jnp.float32,
    )


def pack_half(panel, inverse_columns, names):
    sections, share, width = inverse_columns.shape
    parts = 2
    lanes = width // parts

    def kernel(where_ref, *refs):
        panel_refs, inverse_ref, out_ref = refs[:-2], refs[-2], refs[-1]
        for i, (j, k) in enumerate(names):
            if j == k:
                out_ref[i] = inverse_ref[k]
            else:
                out_ref[i] = panel_refs[k][j * share : (j + 1) * share, :]

    panel_specs = [
        pl.BlockSpec((sections * share, lanes), lambda i, where, k=k: (0, k * parts + where[0]))
        for k in range(sections - 1)
    ]
    return pl.pallas_call(
        kernel,
        out_shape=jax.ShapeDtypeStruct((len(names), share, lanes), jnp.float32),
        grid_spec=pltpu.PrefetchScalarGridSpec(
            num_scalar_prefetch=1,
            grid=(1,),
            in_specs=panel_specs
            + [pl.BlockSpec((sections, share, lanes), lambda i, where: (0, 0, where[0]))],
            out_specs=pl.BlockSpec((len(names), share, lanes), lambda i, where: (0, 0, 0)),
        ),
    )((lax.axis_index("rhs") % 2).astype(jnp.int32)[None], *[panel] * (sections - 1), inverse_columns)


def join_lanes(near, far):
    low = lax.axis_index("rhs") % 2 == 0
    return jnp.concatenate([jnp.where(low, near, far), jnp.where(low, far, near)], axis=2)


def redistribute(targets, send_order, send_count, recv_slot):
    groups = lax.axis_size(ROWS)
    arrived = lax.all_to_all(targets, "rhs", split_axis=1, concat_axis=0, tiled=True)
    rows_local, columns = arrived.shape
    capacity, tag = 4, 64
    counts = send_count[0]
    dest = jnp.arange(groups, dtype=jnp.int32)
    starts = jnp.sum(jnp.where(dest[None, :] < dest[:, None], counts[None, :], 0), axis=1)
    index = jnp.arange(rows_local, dtype=jnp.int32)
    position = jnp.sum(jnp.where(send_order[:, None] == index[None, :], index[:, None], 0), axis=0)
    slot_number = jnp.arange(capacity, dtype=jnp.int32)
    listed = starts[None, :] + slot_number[:, None]
    listed = jnp.where(slot_number[:, None] < counts[None, :], listed, -1)
    picked = (listed[:, :, None] == position[None, None, :]).astype(jnp.float32)
    picked = picked.reshape(capacity * groups, rows_local)
    landing = jnp.broadcast_to((recv_slot + 1).astype(jnp.float32)[:, None], (rows_local, 2 * tag))
    planes = product(picked, jnp.concatenate([arrived, landing], axis=1))
    planes = planes.reshape(capacity, groups, columns + 2 * tag)
    halves = [
        jnp.concatenate(
            [
                planes[s, :, :columns],
                planes[s + 1, :, :columns],
                planes[s, :, columns : columns + tag],
                planes[s + 1, :, columns : columns + tag],
            ],
            axis=1,
        )
        for s in range(0, capacity, 2)
    ]
    incoming = lax.all_to_all(
        jnp.stack(halves, axis=1), ROWS, split_axis=0, concat_axis=0, tiled=True
    )
    total = 0.0
    for h in range(capacity // 2):
        half = incoming[:, h]
        for s in range(2):
            label = half[:, 2 * columns + s * tag : 2 * columns + s * tag + 1] - 1.0
            placed = (label.astype(jnp.int32) == index[None, :]).astype(jnp.float32)
            rows = half[:, s * columns : (s + 1) * columns]
            total = total + product(placed, rows, ((0,), (0,)))
    return total


def whole_block(mine, first):
    other = lax.ppermute(mine, "core", SWAP)
    both = jnp.stack([jnp.where(first, mine, other), jnp.where(first, other, mine)], axis=1)
    return both.reshape(2 * mine.shape[0] * mine.shape[1], mine.shape[2])


def shards(targets, send_order, send_count, recv_slot, panel, inv_diag):
    sections, block_rows, share = inv_diag.shape
    nx, nz, nc = (lax.axis_size(a) for a in ROWS)
    zi = lax.axis_index("z")
    first = lax.axis_index("core") == 0
    even = zi % 2 == 0
    square = sections * share
    inverse_columns = jnp.swapaxes(inv_diag, 1, 2)

    weight = {}
    names = [(j, k) for j in range(sections) for k in range(j + 1)]
    some_lanes = lax.all_gather(pack_half(panel, inverse_columns, names), "z")
    residual = redistribute(targets, send_order, send_count, recv_slot)
    cuts = [0, 2, 5, len(names)]
    batches, order = [], None
    for low, high in zip(cuts, cuts[1:]):
        near = some_lanes[:, low:high].transpose(1, 0, 2, 3)
        near = near.reshape(high - low, nz * share, some_lanes.shape[3])
        if order is not None:
            order, near = lax.optimization_barrier((order, near))
        order = [near, lax.ppermute(near, "rhs", [(i, i ^ 1) for i in range(lax.axis_size("rhs"))])]
        batches.append(order)

    def unpack(batch):
        for name, tile in zip(names[cuts[batch] : cuts[batch + 1]], join_lanes(*batches[batch])):
            weight[name] = tile

    unpack(0)

    columns = residual.shape[1] // 2
    halves = jnp.stack([residual[:square, :columns], residual[:square, columns:]])
    tops = jnp.broadcast_to(halves[None], (nz // 2,) + halves.shape).reshape(nz, square, columns)
    tops = lax.all_to_all(tops, "z", split_axis=0, concat_axis=0, tiled=True)
    pending = [
        tops[:, k * share : (k + 1) * share].reshape(nz * share, columns) for k in range(sections)
    ]
    left, right = residual[square:, :columns], residual[square:, columns:]
    below = [jnp.where(even, left, right), jnp.where(even, right, left)]
    start = ((lax.axis_index("x") * nz + zi) * nc + lax.axis_index("core")) * share
    finished, blocks, used = [], [], set()
    for k in range(sections):
        partial = product(weight[(k, k)], pending[k], ((0,), (0,)))
        partial = partial.reshape(nx * nz, nc, share, columns)
        keep = jnp.where(first, partial[:, 0], partial[:, 1])
        give = jnp.where(first, partial[:, 1], partial[:, 0])
        half = keep + lax.ppermute(give, "core", SWAP)
        copies = jnp.broadcast_to(half[None], (nx,) + half.shape)
        mine = jnp.sum(lax.all_to_all(copies, "x", split_axis=0, concat_axis=0, tiled=True), axis=0)
        solved = whole_block(mine, first)
        blocks.append(solved)
        if k < 2:
            batches[k + 1] = lax.optimization_barrier((mine, batches[k + 1]))[1]
            unpack(k + 1)
        for j, i in sorted(weight):
            if j > i and i <= k and (j, i) not in used:
                pending[j] = pending[j] - product(weight[(j, i)], blocks[i])
                used.add((j, i))
        trade = [(i, i ^ 1) for i in range(nz)]
        if k + 1 < sections:
            traded = lax.ppermute(solved, "z", trade)
        else:
            traded = whole_block(lax.ppermute(mine, "z", trade), first)
        factor = panel[square:, k * block_rows : (k + 1) * block_rows]
        pieces = []
        for h, block in enumerate((solved, traded)):
            below[h] = below[h] - product(factor, block)
            pieces.append(lax.dynamic_slice_in_dim(block, start, share, 0))
        finished.append(pieces)
    ends = [jnp.concatenate([f[h] for f in finished] + [below[h]], axis=0) for h in range(2)]
    return jnp.concatenate(
        [jnp.where(even, ends[0], ends[1]), jnp.where(even, ends[1], ends[0])], axis=1
    )


def solution(mesh):
    ny = mesh.shape["rhs"]
    split = Mesh(mesh.devices.reshape(4, 16, 2, ny), ROWS + ("rhs",))
    placed = (
        P(ROWS + ("rhs",), None),
        P(ROWS),
        P(ROWS, None),
        P(ROWS),
        P(ROWS, None),
        P(None, None, ROWS),
    )
    return jax.shard_map(
        shards, mesh=split, in_specs=placed, out_specs=P(ROWS, "rhs"), check_vma=False
    )
```

```python
import jax
import jax.numpy as jnp
from jax import lax
from jax.experimental import pallas as pl
from jax.sharding import Mesh, PartitionSpec as P

ROWS = ("x", "z", "core")
SWAP = [(0, 1), (1, 0)]


def product(left, right, contract=((1,), (0,))):
    return lax.dot_general(
        left,
        right,
        (contract, ((), ())),
        precision=lax.Precision.HIGHEST,
        preferred_element_type=jnp.float32,
    )


def pack_tiles(panel, inverse_columns, batches):
    sections, share, width = inverse_columns.shape

    def kernel(panel_ref, inverse_ref, *out_refs):
        for out_ref, names in zip(out_refs, batches):
            for i, (j, k) in enumerate(names):
                if j == k:
                    out_ref[i] = inverse_ref[k]
                else:
                    out_ref[i] = panel_ref[j * share : (j + 1) * share, k * width : (k + 1) * width]

    return pl.pallas_call(
        kernel,
        grid=(1,),
        out_shape=[jax.ShapeDtypeStruct((len(b), share, width), jnp.float32) for b in batches],
        in_specs=[
            pl.BlockSpec((sections * share, (sections - 1) * width), lambda i: (0, 0)),
            pl.BlockSpec((sections, share, width), lambda i: (0, 0, 0)),
        ],
        out_specs=[pl.BlockSpec((len(b), share, width), lambda i: (0, 0, 0)) for b in batches],
    )(panel, inverse_columns)


def redistribute(targets, send_order, send_count, recv_slot):
    groups = lax.axis_size(ROWS)
    arrived = lax.all_to_all(targets, "rhs", split_axis=1, concat_axis=0, tiled=True)
    rows_local, columns = arrived.shape
    capacity, tag = 4, 64
    counts = send_count[0]
    dest = jnp.arange(groups, dtype=jnp.int32)
    starts = jnp.sum(jnp.where(dest[None, :] < dest[:, None], counts[None, :], 0), axis=1)
    index = jnp.arange(rows_local, dtype=jnp.int32)
    position = jnp.sum(jnp.where(send_order[:, None] == index[None, :], index[:, None], 0), axis=0)
    slot_number = jnp.arange(capacity, dtype=jnp.int32)
    listed = starts[None, :] + slot_number[:, None]
    listed = jnp.where(slot_number[:, None] < counts[None, :], listed, -1)
    picked = (listed[:, :, None] == position[None, None, :]).astype(jnp.float32)
    picked = picked.reshape(capacity * groups, rows_local)
    landing = jnp.broadcast_to((recv_slot + 1).astype(jnp.float32)[:, None], (rows_local, 2 * tag))
    planes = product(picked, jnp.concatenate([arrived, landing], axis=1))
    planes = planes.reshape(capacity, groups, columns + 2 * tag)
    halves = [
        jnp.concatenate(
            [
                planes[s, :, :columns],
                planes[s + 1, :, :columns],
                planes[s, :, columns : columns + tag],
                planes[s + 1, :, columns : columns + tag],
            ],
            axis=1,
        )
        for s in range(0, capacity, 2)
    ]
    incoming = lax.all_to_all(
        jnp.stack(halves, axis=1), ROWS, split_axis=0, concat_axis=0, tiled=True
    )
    total = 0.0
    for h in range(capacity // 2):
        half = incoming[:, h]
        for s in range(2):
            label = half[:, 2 * columns + s * tag : 2 * columns + s * tag + 1] - 1.0
            placed = (label.astype(jnp.int32) == index[None, :]).astype(jnp.float32)
            rows = half[:, s * columns : (s + 1) * columns]
            total = total + product(placed, rows, ((0,), (0,)))
    return total


def whole_block(mine, first):
    other = lax.ppermute(mine, "core", SWAP)
    both = jnp.stack([jnp.where(first, mine, other), jnp.where(first, other, mine)], axis=1)
    return both.reshape(2 * mine.shape[0] * mine.shape[1], mine.shape[2])


def shards(targets, send_order, send_count, recv_slot, panel, inv_diag):
    sections, block_rows, share = inv_diag.shape
    nx, nz, nc = (lax.axis_size(a) for a in ROWS)
    zi = lax.axis_index("z")
    first = lax.axis_index("core") == 0
    even = zi % 2 == 0
    square = sections * share
    inverse_columns = jnp.swapaxes(inv_diag, 1, 2)

    weight = {}
    names = [(j, k) for j in range(sections) for k in range(j + 1)]
    (tiles,) = pack_tiles(panel, inverse_columns, [names])
    gathered = lax.all_gather(tiles, "z")
    for i, name in enumerate(names):
        weight[name] = gathered[:, i].reshape(nz * share, block_rows)

    residual = redistribute(targets, send_order, send_count, recv_slot)
    columns = residual.shape[1] // 2
    halves = jnp.stack([residual[:square, :columns], residual[:square, columns:]])
    tops = jnp.broadcast_to(halves[None], (nz // 2,) + halves.shape).reshape(nz, square, columns)
    tops = lax.all_to_all(tops, "z", split_axis=0, concat_axis=0, tiled=True)
    pending = [
        tops[:, k * share : (k + 1) * share].reshape(nz * share, columns) for k in range(sections)
    ]
    left, right = residual[square:, :columns], residual[square:, columns:]
    below = [jnp.where(even, left, right), jnp.where(even, right, left)]
    start = ((lax.axis_index("x") * nz + zi) * nc + lax.axis_index("core")) * share
    finished = []
    for k in range(sections):
        partial = product(weight[(k, k)], pending[k], ((0,), (0,)))
        partial = partial.reshape(nx * nz, nc, share, columns)
        keep = jnp.where(first, partial[:, 0], partial[:, 1])
        give = jnp.where(first, partial[:, 1], partial[:, 0])
        half = keep + lax.ppermute(give, "core", SWAP)
        copies = jnp.broadcast_to(half[None], (nx,) + half.shape)
        mine = jnp.sum(lax.all_to_all(copies, "x", split_axis=0, concat_axis=0, tiled=True), axis=0)
        solved = whole_block(mine, first)
        for j in range(k + 1, sections):
            pending[j] = pending[j] - product(weight[(j, k)], solved)
        trade = [(i, i ^ 1) for i in range(nz)]
        if k + 1 < sections:
            traded = lax.ppermute(solved, "z", trade)
        else:
            traded = whole_block(lax.ppermute(mine, "z", trade), first)
        factor = panel[square:, k * block_rows : (k + 1) * block_rows]
        pieces = []
        for h, block in enumerate((solved, traded)):
            below[h] = below[h] - product(factor, block)
            pieces.append(lax.dynamic_slice_in_dim(block, start, share, 0))
        finished.append(pieces)
    ends = [jnp.concatenate([f[h] for f in finished] + [below[h]], axis=0) for h in range(2)]
    return jnp.concatenate(
        [jnp.where(even, ends[0], ends[1]), jnp.where(even, ends[1], ends[0])], axis=1
    )


def solution(mesh):
    ny = mesh.shape["rhs"]
    split = Mesh(mesh.devices.reshape(4, 16, 2, ny), ROWS + ("rhs",))
    placed = (
        P(ROWS + ("rhs",), None),
        P(ROWS),
        P(ROWS, None),
        P(ROWS),
        P(ROWS, None),
        P(None, None, ROWS),
    )
    return jax.shard_map(
        shards, mesh=split, in_specs=placed, out_specs=P(ROWS, "rhs"), check_vma=False
    )
```

```python
import jax
import jax.numpy as jnp
from jax import lax
from jax.experimental import pallas as pl
from jax.sharding import Mesh, PartitionSpec as P

ROWS = ("x", "z", "core")
SWAP = [(0, 1), (1, 0)]


def product(left, right, contract=((1,), (0,))):
    return lax.dot_general(
        left,
        right,
        (contract, ((), ())),
        precision=lax.Precision.HIGHEST,
        preferred_element_type=jnp.float32,
    )


def pack_tiles(panel, inverse_columns, batches):
    sections, share, width = inverse_columns.shape

    def kernel(panel_ref, inverse_ref, *out_refs):
        for out_ref, names in zip(out_refs, batches):
            for i, (j, k) in enumerate(names):
                if j == k:
                    out_ref[i] = inverse_ref[k]
                else:
                    out_ref[i] = panel_ref[j * share : (j + 1) * share, k * width : (k + 1) * width]

    return pl.pallas_call(
        kernel,
        grid=(1,),
        out_shape=[jax.ShapeDtypeStruct((len(b), share, width), jnp.float32) for b in batches],
        in_specs=[
            pl.BlockSpec((sections * share, (sections - 1) * width), lambda i: (0, 0)),
            pl.BlockSpec((sections, share, width), lambda i: (0, 0, 0)),
        ],
        out_specs=[pl.BlockSpec((len(b), share, width), lambda i: (0, 0, 0)) for b in batches],
    )(panel, inverse_columns)


def redistribute(targets, send_order, send_count, recv_slot):
    groups = lax.axis_size(ROWS)
    arrived = lax.all_to_all(targets, "rhs", split_axis=1, concat_axis=0, tiled=True)
    rows_local, columns = arrived.shape
    capacity, tag = 4, 64
    counts = send_count[0]
    dest = jnp.arange(groups, dtype=jnp.int32)
    starts = jnp.sum(jnp.where(dest[None, :] < dest[:, None], counts[None, :], 0), axis=1)
    index = jnp.arange(rows_local, dtype=jnp.int32)
    position = jnp.sum(jnp.where(send_order[:, None] == index[None, :], index[:, None], 0), axis=0)
    slot_number = jnp.arange(capacity, dtype=jnp.int32)
    listed = starts[None, :] + slot_number[:, None]
    listed = jnp.where(slot_number[:, None] < counts[None, :], listed, -1)
    picked = (listed[:, :, None] == position[None, None, :]).astype(jnp.float32)
    picked = picked.reshape(capacity * groups, rows_local)
    landing = jnp.broadcast_to((recv_slot + 1).astype(jnp.float32)[:, None], (rows_local, 2 * tag))
    planes = product(picked, jnp.concatenate([arrived, landing], axis=1))
    planes = planes.reshape(capacity, groups, columns + 2 * tag)
    halves = [
        jnp.concatenate(
            [
                planes[s, :, :columns],
                planes[s + 1, :, :columns],
                planes[s, :, columns : columns + tag],
                planes[s + 1, :, columns : columns + tag],
            ],
            axis=1,
        )
        for s in range(0, capacity, 2)
    ]
    incoming = lax.all_to_all(
        jnp.stack(halves, axis=1), ROWS, split_axis=0, concat_axis=0, tiled=True
    )
    total = 0.0
    for h in range(capacity // 2):
        half = incoming[:, h]
        for s in range(2):
            label = half[:, 2 * columns + s * tag : 2 * columns + s * tag + 1] - 1.0
            placed = (label.astype(jnp.int32) == index[None, :]).astype(jnp.float32)
            rows = half[:, s * columns : (s + 1) * columns]
            total = total + product(placed, rows, ((0,), (0,)))
    return total


def whole_block(mine, first):
    other = lax.ppermute(mine, "core", SWAP)
    both = jnp.stack([jnp.where(first, mine, other), jnp.where(first, other, mine)], axis=1)
    return both.reshape(2 * mine.shape[0] * mine.shape[1], mine.shape[2])


def shards(targets, send_order, send_count, recv_slot, panel, inv_diag):
    sections, block_rows, share = inv_diag.shape
    nx, nz, nc = (lax.axis_size(a) for a in ROWS)
    zi = lax.axis_index("z")
    first = lax.axis_index("core") == 0
    even = zi % 2 == 0
    square = sections * share
    inverse_columns = jnp.swapaxes(inv_diag, 1, 2)

    weight = {}
    names = [(j, k) for j in range(sections) for k in range(j + 1)]
    (tiles,) = pack_tiles(panel, inverse_columns, [names])
    gathered = lax.all_gather(tiles, "z")
    for i, name in enumerate(names):
        weight[name] = gathered[:, i].reshape(nz * share, block_rows)

    residual = redistribute(targets, send_order, send_count, recv_slot)
    columns = residual.shape[1] // 2
    halves = jnp.stack([residual[:square, :columns], residual[:square, columns:]])
    tops = jnp.broadcast_to(halves[None], (nz // 2,) + halves.shape).reshape(nz, square, columns)
    tops = lax.all_to_all(tops, "z", split_axis=0, concat_axis=0, tiled=True)
    pending = [
        tops[:, k * share : (k + 1) * share].reshape(nz * share, columns) for k in range(sections)
    ]
    left, right = residual[square:, :columns], residual[square:, columns:]
    below = [jnp.where(even, left, right), jnp.where(even, right, left)]
    start = ((lax.axis_index("x") * nz + zi) * nc + lax.axis_index("core")) * share
    finished, later = [[], []], []

    def update(side, k, block):
        factor = panel[square:, k * block_rows : (k + 1) * block_rows]
        below[side] = below[side] - product(factor, block)
        finished[side].append(lax.dynamic_slice_in_dim(block, start, share, 0))

    for k in range(sections):
        partial = product(weight[(k, k)], pending[k], ((0,), (0,)))
        partial = partial.reshape(nx * nz, nc, share, columns)
        keep = jnp.where(first, partial[:, 0], partial[:, 1])
        give = jnp.where(first, partial[:, 1], partial[:, 0])
        half = keep + lax.ppermute(give, "core", SWAP)
        copies = jnp.broadcast_to(half[None], (nx,) + half.shape)
        mine = jnp.sum(lax.all_to_all(copies, "x", split_axis=0, concat_axis=0, tiled=True), axis=0)
        solved = whole_block(mine, first)
        for j in range(k + 1, sections):
            pending[j] = pending[j] - product(weight[(j, k)], solved)
        trade = [(i, i ^ 1) for i in range(nz)]
        if k + 1 < sections:
            traded = lax.ppermute(solved, "z", trade)
        else:
            traded = whole_block(lax.ppermute(mine, "z", trade), first)
        update(0, k, solved)
        later.append((k, traded))
        while later and (later[0][0] + 2 <= k or k + 1 == sections):
            old, block = later.pop(0)
            if old < k:
                block = lax.optimization_barrier((mine, block))[1]
            update(1, old, block)
    ends = [jnp.concatenate(finished[h] + [below[h]], axis=0) for h in range(2)]
    return jnp.concatenate(
        [jnp.where(even, ends[0], ends[1]), jnp.where(even, ends[1], ends[0])], axis=1
    )


def solution(mesh):
    ny = mesh.shape["rhs"]
    split = Mesh(mesh.devices.reshape(4, 16, 2, ny), ROWS + ("rhs",))
    placed = (
        P(ROWS + ("rhs",), None),
        P(ROWS),
        P(ROWS, None),
        P(ROWS),
        P(ROWS, None),
        P(None, None, ROWS),
    )
    return jax.shard_map(
        shards, mesh=split, in_specs=placed, out_specs=P(ROWS, "rhs"), check_vma=False
    )
```

```python
import jax
import jax.numpy as jnp
from jax import lax
from jax.experimental import pallas as pl
from jax.sharding import Mesh, PartitionSpec as P

ROWS = ("x", "z", "core")
SWAP = [(0, 1), (1, 0)]


def product(left, right, contract=((1,), (0,))):
    return lax.dot_general(
        left,
        right,
        (contract, ((), ())),
        precision=lax.Precision.HIGHEST,
        preferred_element_type=jnp.float32,
    )


def pack_tiles(panel, inverse_columns, batches):
    sections, share, width = inverse_columns.shape

    def kernel(panel_ref, inverse_ref, *out_refs):
        for out_ref, names in zip(out_refs, batches):
            for i, (j, k) in enumerate(names):
                if j == k:
                    out_ref[i] = inverse_ref[k]
                else:
                    out_ref[i] = panel_ref[j * share : (j + 1) * share, k * width : (k + 1) * width]

    return pl.pallas_call(
        kernel,
        grid=(1,),
        out_shape=[jax.ShapeDtypeStruct((len(b), share, width), jnp.float32) for b in batches],
        in_specs=[
            pl.BlockSpec((sections * share, (sections - 1) * width), lambda i: (0, 0)),
            pl.BlockSpec((sections, share, width), lambda i: (0, 0, 0)),
        ],
        out_specs=[pl.BlockSpec((len(b), share, width), lambda i: (0, 0, 0)) for b in batches],
    )(panel, inverse_columns)


def redistribute(targets, send_order, send_count, recv_slot):
    groups = lax.axis_size(ROWS)
    arrived = lax.all_to_all(targets, "rhs", split_axis=1, concat_axis=0, tiled=True)
    rows_local, columns = arrived.shape
    capacity, tag = 4, 32
    counts = send_count[0]
    dest = jnp.arange(groups, dtype=jnp.int32)
    starts = jnp.sum(jnp.where(dest[None, :] < dest[:, None], counts[None, :], 0), axis=1)
    index = jnp.arange(rows_local, dtype=jnp.int32)
    position = jnp.sum(jnp.where(send_order[:, None] == index[None, :], index[:, None], 0), axis=0)
    slot_number = jnp.arange(capacity, dtype=jnp.int32)
    listed = starts[None, :] + slot_number[:, None]
    listed = jnp.where(slot_number[:, None] < counts[None, :], listed, -1)
    picked = (listed[:, :, None] == position[None, None, :]).astype(jnp.float32)
    picked = picked.reshape(capacity * groups, rows_local)
    landing = jnp.broadcast_to((recv_slot + 1).astype(jnp.float32)[:, None], (rows_local, tag * capacity))
    planes = product(picked, jnp.concatenate([arrived, landing], axis=1))
    planes = planes.reshape(capacity, groups, columns + tag * capacity)
    sent = jnp.concatenate(
        [planes[s, :, :columns] for s in range(capacity)]
        + [planes[s, :, columns + s * tag : columns + (s + 1) * tag] for s in range(capacity)],
        axis=1,
    )
    incoming = lax.all_to_all(
        sent[:, None], ROWS, split_axis=0, concat_axis=0, tiled=True
    )[:, 0]
    total = 0.0
    for s in range(capacity):
        spot = capacity * columns + s * tag
        label = incoming[:, spot : spot + 1] - 1.0
        placed = (label.astype(jnp.int32) == index[None, :]).astype(jnp.float32)
        rows = incoming[:, s * columns : (s + 1) * columns]
        total = total + product(placed, rows, ((0,), (0,)))
    return total


def whole_block(mine, first):
    other = lax.ppermute(mine, "core", SWAP)
    both = jnp.stack([jnp.where(first, mine, other), jnp.where(first, other, mine)], axis=1)
    return both.reshape(2 * mine.shape[0] * mine.shape[1], mine.shape[2])


def shards(targets, send_order, send_count, recv_slot, panel, inv_diag):
    sections, block_rows, share = inv_diag.shape
    nx, nz, nc = (lax.axis_size(a) for a in ROWS)
    zi = lax.axis_index("z")
    first = lax.axis_index("core") == 0
    even = zi % 2 == 0
    square = sections * share
    inverse_columns = jnp.swapaxes(inv_diag, 1, 2)

    weight = {}
    names = [(j, k) for j in range(sections) for k in range(j + 1)]
    (tiles,) = pack_tiles(panel, inverse_columns, [names])
    gathered = lax.all_gather(tiles, "z")
    for i, name in enumerate(names):
        weight[name] = gathered[:, i].reshape(nz * share, block_rows)

    residual = redistribute(targets, send_order, send_count, recv_slot)
    columns = residual.shape[1] // 2
    halves = jnp.stack([residual[:square, :columns], residual[:square, columns:]])
    tops = jnp.broadcast_to(halves[None], (nz // 2,) + halves.shape).reshape(nz, square, columns)
    tops = lax.all_to_all(tops, "z", split_axis=0, concat_axis=0, tiled=True)
    pending = [
        tops[:, k * share : (k + 1) * share].reshape(nz * share, columns) for k in range(sections)
    ]
    left, right = residual[square:, :columns], residual[square:, columns:]
    below = [jnp.where(even, left, right), jnp.where(even, right, left)]
    start = ((lax.axis_index("x") * nz + zi) * nc + lax.axis_index("core")) * share
    finished, later = [[], []], []

    def update(side, k, block):
        factor = panel[square:, k * block_rows : (k + 1) * block_rows]
        below[side] = below[side] - product(factor, block)
        finished[side].append(lax.dynamic_slice_in_dim(block, start, share, 0))

    for k in range(sections):
        partial = product(weight[(k, k)], pending[k], ((0,), (0,)))
        partial = partial.reshape(nx * nz, nc, share, columns)
        keep = jnp.where(first, partial[:, 0], partial[:, 1])
        give = jnp.where(first, partial[:, 1], partial[:, 0])
        half = keep + lax.ppermute(give, "core", SWAP)
        copies = jnp.broadcast_to(half[None], (nx,) + half.shape)
        mine = jnp.sum(lax.all_to_all(copies, "x", split_axis=0, concat_axis=0, tiled=True), axis=0)
        solved = whole_block(mine, first)
        for j in range(k + 1, sections):
            pending[j] = pending[j] - product(weight[(j, k)], solved)
        trade = [(i, i ^ 1) for i in range(nz)]
        if k + 1 < sections:
            traded = lax.ppermute(solved, "z", trade)
        else:
            traded = whole_block(lax.ppermute(mine, "z", trade), first)
        update(0, k, solved)
        later.append((k, traded))
        while later and (later[0][0] + 2 <= k or k + 1 == sections):
            old, block = later.pop(0)
            if old < k:
                block = lax.optimization_barrier((mine, block))[1]
            update(1, old, block)
    ends = [jnp.concatenate(finished[h] + [below[h]], axis=0) for h in range(2)]
    return jnp.concatenate(
        [jnp.where(even, ends[0], ends[1]), jnp.where(even, ends[1], ends[0])], axis=1
    )


def solution(mesh):
    ny = mesh.shape["rhs"]
    split = Mesh(mesh.devices.reshape(4, 16, 2, ny), ROWS + ("rhs",))
    placed = (
        P(ROWS + ("rhs",), None),
        P(ROWS),
        P(ROWS, None),
        P(ROWS),
        P(ROWS, None),
        P(None, None, ROWS),
    )
    return jax.shard_map(
        shards, mesh=split, in_specs=placed, out_specs=P(ROWS, "rhs"), check_vma=False
    )
```

```python
import jax
import jax.numpy as jnp
from jax import lax
from jax.experimental import pallas as pl
from jax.sharding import Mesh, PartitionSpec as P

ROWS = ("x", "z", "core")
SWAP = [(0, 1), (1, 0)]


def product(left, right, contract=((1,), (0,))):
    return lax.dot_general(
        left,
        right,
        (contract, ((), ())),
        precision=lax.Precision.HIGHEST,
        preferred_element_type=jnp.float32,
    )


def pack_tiles(panel, inverse_columns, batches):
    sections, share, width = inverse_columns.shape

    def kernel(panel_ref, inverse_ref, *out_refs):
        for out_ref, names in zip(out_refs, batches):
            for i, (j, k) in enumerate(names):
                if j == k:
                    out_ref[i] = inverse_ref[k]
                else:
                    out_ref[i] = panel_ref[j * share : (j + 1) * share, k * width : (k + 1) * width]

    return pl.pallas_call(
        kernel,
        grid=(1,),
        out_shape=[jax.ShapeDtypeStruct((len(b), share, width), jnp.float32) for b in batches],
        in_specs=[
            pl.BlockSpec((sections * share, (sections - 1) * width), lambda i: (0, 0)),
            pl.BlockSpec((sections, share, width), lambda i: (0, 0, 0)),
        ],
        out_specs=[pl.BlockSpec((len(b), share, width), lambda i: (0, 0, 0)) for b in batches],
    )(panel, inverse_columns)


def redistribute(targets, send_order, send_count, recv_slot):
    groups = lax.axis_size(ROWS)
    arrived = lax.all_to_all(targets, "rhs", split_axis=1, concat_axis=0, tiled=True)
    rows_local, columns = arrived.shape
    capacity, tag = 4, 32
    counts = send_count[0]
    dest = jnp.arange(groups, dtype=jnp.int32)
    starts = jnp.sum(jnp.where(dest[None, :] < dest[:, None], counts[None, :], 0), axis=1)
    index = jnp.arange(rows_local, dtype=jnp.int32)
    position = jnp.sum(jnp.where(send_order[:, None] == index[None, :], index[:, None], 0), axis=0)
    slot_number = jnp.arange(capacity, dtype=jnp.int32)
    listed = starts[None, :] + slot_number[:, None]
    listed = jnp.where(slot_number[:, None] < counts[None, :], listed, -1)
    picked = (listed[:, :, None] == position[None, None, :]).astype(jnp.float32)
    picked = picked.reshape(capacity * groups, rows_local)
    landing = jnp.broadcast_to((recv_slot + 1).astype(jnp.float32)[:, None], (rows_local, tag * capacity))
    planes = product(picked, jnp.concatenate([arrived, landing], axis=1))
    planes = planes.reshape(capacity, groups, columns + tag * capacity)
    sent = jnp.concatenate(
        [planes[s, :, :columns] for s in range(capacity)]
        + [planes[s, :, columns + s * tag : columns + (s + 1) * tag] for s in range(capacity)],
        axis=1,
    )
    incoming = lax.all_to_all(
        sent[:, None], ROWS, split_axis=0, concat_axis=0, tiled=True
    )[:, 0]
    total = 0.0
    for s in range(capacity):
        spot = capacity * columns + s * tag
        label = incoming[:, spot : spot + 1] - 1.0
        placed = (label.astype(jnp.int32) == index[None, :]).astype(jnp.float32)
        rows = incoming[:, s * columns : (s + 1) * columns]
        total = total + product(placed, rows, ((0,), (0,)))
    return total


def whole_block(mine, other, first):
    both = jnp.stack([jnp.where(first, mine, other), jnp.where(first, other, mine)], axis=1)
    return both.reshape(2 * mine.shape[0] * mine.shape[1], mine.shape[2])


def shards(targets, send_order, send_count, recv_slot, panel, inv_diag):
    sections, block_rows, share = inv_diag.shape
    nx, nz, nc = (lax.axis_size(a) for a in ROWS)
    zi = lax.axis_index("z")
    first = lax.axis_index("core") == 0
    even = zi % 2 == 0
    square = sections * share
    inverse_columns = jnp.swapaxes(inv_diag, 1, 2)

    weight = {}
    names = [(j, k) for j in range(sections) for k in range(j + 1)]
    (tiles,) = pack_tiles(panel, inverse_columns, [names])
    lane = jnp.arange(block_rows, dtype=jnp.int32)
    apart = (lane // share % nc != lax.axis_index("core")).astype(jnp.int32)
    moved = apart * (block_rows // nc) + lane // (nc * share) * share + lane % share
    order = (moved[:, None] == lane[None, :]).astype(jnp.float32)
    tiles = product(tiles.reshape(len(names) * share, block_rows), order).reshape(tiles.shape)
    gathered = lax.all_gather(tiles, "z")
    for i, name in enumerate(names):
        weight[name] = gathered[:, i].reshape(nz * share, block_rows)

    residual = redistribute(targets, send_order, send_count, recv_slot)
    columns = residual.shape[1] // 2
    halves = jnp.stack([residual[:square, :columns], residual[:square, columns:]])
    tops = jnp.broadcast_to(halves[None], (nz // 2,) + halves.shape).reshape(nz, square, columns)
    tops = lax.all_to_all(tops, "z", split_axis=0, concat_axis=0, tiled=True)
    pending = [
        tops[:, k * share : (k + 1) * share].reshape(nz * share, columns) for k in range(sections)
    ]
    left, right = residual[square:, :columns], residual[square:, columns:]
    below = [jnp.where(even, left, right), jnp.where(even, right, left)]
    start = ((lax.axis_index("x") * nz + zi) * nc + lax.axis_index("core")) * share
    finished, later = [[], []], []

    def update(side, k, block):
        factor = panel[square:, k * block_rows : (k + 1) * block_rows]
        below[side] = below[side] - product(factor, block)
        finished[side].append(lax.dynamic_slice_in_dim(block, start, share, 0))

    for k in range(sections):
        partial = product(weight[(k, k)], pending[k], ((0,), (0,)))
        partial = partial.reshape(nc, nx * nz, share, columns)
        half = partial[0] + lax.ppermute(partial[1], "core", SWAP)
        copies = jnp.broadcast_to(half[None], (nx,) + half.shape)
        mine = jnp.sum(lax.all_to_all(copies, "x", split_axis=0, concat_axis=0, tiled=True), axis=0)
        other = lax.ppermute(mine, "core", SWAP)
        apart = jnp.concatenate([mine, other], axis=0).reshape(block_rows, columns)
        solved = whole_block(mine, other, first)
        for j in range(k + 1, sections):
            pending[j] = pending[j] - product(weight[(j, k)], apart)
        trade = [(i, i ^ 1) for i in range(nz)]
        if k + 1 < sections:
            traded = lax.ppermute(solved, "z", trade)
        else:
            traded = lax.ppermute(mine, "z", trade)
            traded = whole_block(traded, lax.ppermute(traded, "core", SWAP), first)
        update(0, k, solved)
        later.append((k, traded))
        while later and (later[0][0] + 2 <= k or k + 1 == sections):
            old, block = later.pop(0)
            if old < k:
                block = lax.optimization_barrier((mine, block))[1]
            update(1, old, block)
    ends = [jnp.concatenate(finished[h] + [below[h]], axis=0) for h in range(2)]
    return jnp.concatenate(
        [jnp.where(even, ends[0], ends[1]), jnp.where(even, ends[1], ends[0])], axis=1
    )


def solution(mesh):
    ny = mesh.shape["rhs"]
    split = Mesh(mesh.devices.reshape(4, 16, 2, ny), ROWS + ("rhs",))
    placed = (
        P(ROWS + ("rhs",), None),
        P(ROWS),
        P(ROWS, None),
        P(ROWS),
        P(ROWS, None),
        P(None, None, ROWS),
    )
    return jax.shard_map(
        shards, mesh=split, in_specs=placed, out_specs=P(ROWS, "rhs"), check_vma=False
    )
```

```python
import jax
import jax.numpy as jnp
from jax import lax
from jax.experimental import pallas as pl
from jax.sharding import Mesh, PartitionSpec as P

ROWS = ("x", "z", "core")
SWAP = [(0, 1), (1, 0)]


def product(left, right, contract=((1,), (0,))):
    return lax.dot_general(
        left,
        right,
        (contract, ((), ())),
        precision=lax.Precision.HIGHEST,
        preferred_element_type=jnp.float32,
    )


def pack_tiles(panel, inverse_columns, batches):
    sections, share, width = inverse_columns.shape

    def kernel(panel_ref, inverse_ref, *out_refs):
        for out_ref, names in zip(out_refs, batches):
            for i, (j, k) in enumerate(names):
                if j == k:
                    out_ref[i] = inverse_ref[k]
                else:
                    out_ref[i] = panel_ref[j * share : (j + 1) * share, k * width : (k + 1) * width]

    return pl.pallas_call(
        kernel,
        grid=(1,),
        out_shape=[jax.ShapeDtypeStruct((len(b), share, width), jnp.float32) for b in batches],
        in_specs=[
            pl.BlockSpec((sections * share, (sections - 1) * width), lambda i: (0, 0)),
            pl.BlockSpec((sections, share, width), lambda i: (0, 0, 0)),
        ],
        out_specs=[pl.BlockSpec((len(b), share, width), lambda i: (0, 0, 0)) for b in batches],
    )(panel, inverse_columns)


def redistribute(targets, send_order, send_count, recv_slot):
    groups = lax.axis_size(ROWS)
    arrived = lax.all_to_all(targets, "rhs", split_axis=1, concat_axis=0, tiled=True)
    rows_local, columns = arrived.shape
    capacity, tag = 4, 32
    counts = send_count[0]
    dest = jnp.arange(groups, dtype=jnp.int32)
    starts = jnp.sum(jnp.where(dest[None, :] < dest[:, None], counts[None, :], 0), axis=1)
    index = jnp.arange(rows_local, dtype=jnp.int32)
    position = jnp.sum(jnp.where(send_order[:, None] == index[None, :], index[:, None], 0), axis=0)
    slot_number = jnp.arange(capacity, dtype=jnp.int32)
    listed = starts[None, :] + slot_number[:, None]
    listed = jnp.where(slot_number[:, None] < counts[None, :], listed, -1)
    picked = (listed[:, :, None] == position[None, None, :]).astype(jnp.float32)
    picked = picked.reshape(capacity * groups, rows_local)
    landing = jnp.broadcast_to((recv_slot + 1).astype(jnp.float32)[:, None], (rows_local, tag * capacity))
    planes = product(picked, jnp.concatenate([arrived, landing], axis=1))
    planes = planes.reshape(capacity, groups, columns + tag * capacity)
    sent = jnp.concatenate(
        [planes[s, :, :columns] for s in range(capacity)]
        + [planes[s, :, columns + s * tag : columns + (s + 1) * tag] for s in range(capacity)],
        axis=1,
    )
    incoming = lax.all_to_all(
        sent[:, None], ROWS, split_axis=0, concat_axis=0, tiled=True
    )[:, 0]
    total = 0.0
    for s in range(capacity):
        spot = capacity * columns + s * tag
        label = incoming[:, spot : spot + 1] - 1.0
        placed = (label.astype(jnp.int32) == index[None, :]).astype(jnp.float32)
        rows = incoming[:, s * columns : (s + 1) * columns]
        total = total + product(placed, rows, ((0,), (0,)))
    return total


def whole_block(mine, first):
    other = lax.ppermute(mine, "core", SWAP)
    both = jnp.stack([jnp.where(first, mine, other), jnp.where(first, other, mine)], axis=1)
    return both.reshape(2 * mine.shape[0] * mine.shape[1], mine.shape[2])


def shards(targets, send_order, send_count, recv_slot, panel, inv_diag):
    sections, block_rows, share = inv_diag.shape
    nx, nz, nc = (lax.axis_size(a) for a in ROWS)
    zi = lax.axis_index("z")
    first = lax.axis_index("core") == 0
    even = zi % 2 == 0
    square = sections * share
    inverse_columns = jnp.swapaxes(inv_diag, 1, 2)

    weight = {}
    names = [(j, k) for j in range(sections) for k in range(j + 1)]
    (tiles,) = pack_tiles(panel, inverse_columns, [names])
    gathered = lax.all_gather(tiles, "z")
    for i, name in enumerate(names):
        weight[name] = gathered[:, i].reshape(nz * share, block_rows)

    residual = redistribute(targets, send_order, send_count, recv_slot)
    columns = residual.shape[1] // 2
    halves = jnp.stack([residual[:square, :columns], residual[:square, columns:]])
    tops = jnp.broadcast_to(halves[None], (nz // 2,) + halves.shape).reshape(nz, square, columns)
    tops = lax.all_to_all(tops, "z", split_axis=0, concat_axis=0, tiled=True)
    pending = [
        tops[:, k * share : (k + 1) * share].reshape(nz * share, columns) for k in range(sections)
    ]
    left, right = residual[square:, :columns], residual[square:, columns:]
    below = [jnp.where(even, left, right), jnp.where(even, right, left)]
    start = ((lax.axis_index("x") * nz + zi) * nc + lax.axis_index("core")) * share
    finished, later = [[], []], []
    trade = [(i, i ^ 1) for i in range(nz)]

    def update(side, k, block):
        factor = panel[square:, k * block_rows : (k + 1) * block_rows]
        below[side] = below[side] - product(factor, block)
        finished[side].append(lax.dynamic_slice_in_dim(block, start, share, 0))

    for k in range(sections):
        partial = product(weight[(k, k)], pending[k], ((0,), (0,)))
        partial = partial.reshape(nx * nz, nc, share, columns)
        keep = jnp.where(first, partial[:, 0], partial[:, 1])
        give = jnp.where(first, partial[:, 1], partial[:, 0])
        half = keep + lax.ppermute(give, "core", SWAP)
        if k > 0:
            half, previous = lax.optimization_barrier((half, previous))
            later.append((k - 1, lax.ppermute(previous, "z", trade)))
        copies = jnp.broadcast_to(half[None], (nx,) + half.shape)
        mine = jnp.sum(lax.all_to_all(copies, "x", split_axis=0, concat_axis=0, tiled=True), axis=0)
        solved = whole_block(mine, first)
        for j in range(k + 1, sections):
            pending[j] = pending[j] - product(weight[(j, k)], solved)
        update(0, k, solved)
        previous = solved
        if k + 1 == sections:
            later.append((k, whole_block(lax.ppermute(mine, "z", trade), first)))
        while later and (later[0][0] + 2 <= k or k + 1 == sections):
            old, block = later.pop(0)
            if old < k:
                block = lax.optimization_barrier((mine, block))[1]
            update(1, old, block)
    ends = [jnp.concatenate(finished[h] + [below[h]], axis=0) for h in range(2)]
    return jnp.concatenate(
        [jnp.where(even, ends[0], ends[1]), jnp.where(even, ends[1], ends[0])], axis=1
    )


def solution(mesh):
    ny = mesh.shape["rhs"]
    split = Mesh(mesh.devices.reshape(4, 16, 2, ny), ROWS + ("rhs",))
    placed = (
        P(ROWS + ("rhs",), None),
        P(ROWS),
        P(ROWS, None),
        P(ROWS),
        P(ROWS, None),
        P(None, None, ROWS),
    )
    return jax.shard_map(
        shards, mesh=split, in_specs=placed, out_specs=P(ROWS, "rhs"), check_vma=False
    )
```

```python
import jax
import jax.numpy as jnp
from jax import lax
from jax.experimental import pallas as pl
from jax.sharding import Mesh, PartitionSpec as P

ROWS = ("x", "z", "core")
SWAP = [(0, 1), (1, 0)]


def product(left, right, contract=((1,), (0,))):
    return lax.dot_general(
        left,
        right,
        (contract, ((), ())),
        precision=lax.Precision.HIGHEST,
        preferred_element_type=jnp.float32,
    )


def pack_tiles(panel, inverse_columns, batches):
    sections, share, width = inverse_columns.shape

    def kernel(panel_ref, inverse_ref, *out_refs):
        for out_ref, names in zip(out_refs, batches):
            for i, (j, k) in enumerate(names):
                if j == k:
                    out_ref[i] = inverse_ref[k]
                else:
                    out_ref[i] = panel_ref[j * share : (j + 1) * share, k * width : (k + 1) * width]

    return pl.pallas_call(
        kernel,
        grid=(1,),
        out_shape=[jax.ShapeDtypeStruct((len(b), share, width), jnp.float32) for b in batches],
        in_specs=[
            pl.BlockSpec((sections * share, (sections - 1) * width), lambda i: (0, 0)),
            pl.BlockSpec((sections, share, width), lambda i: (0, 0, 0)),
        ],
        out_specs=[pl.BlockSpec((len(b), share, width), lambda i: (0, 0, 0)) for b in batches],
    )(panel, inverse_columns)


def redistribute(targets, send_order, send_count, recv_slot):
    groups = lax.axis_size(ROWS)
    arrived = lax.all_to_all(targets, "rhs", split_axis=1, concat_axis=0, tiled=True)
    rows_local, columns = arrived.shape
    capacity, tag = 4, 32
    counts = send_count[0]
    dest = jnp.arange(groups, dtype=jnp.int32)
    starts = jnp.sum(jnp.where(dest[None, :] < dest[:, None], counts[None, :], 0), axis=1)
    index = jnp.arange(rows_local, dtype=jnp.int32)
    position = jnp.sum(jnp.where(send_order[:, None] == index[None, :], index[:, None], 0), axis=0)
    slot_number = jnp.arange(capacity, dtype=jnp.int32)
    listed = starts[None, :] + slot_number[:, None]
    listed = jnp.where(slot_number[:, None] < counts[None, :], listed, -1)
    picked = (listed[:, :, None] == position[None, None, :]).astype(jnp.float32)
    picked = picked.reshape(capacity * groups, rows_local)
    landing = jnp.broadcast_to((recv_slot + 1).astype(jnp.float32)[:, None], (rows_local, tag * capacity))
    planes = product(picked, jnp.concatenate([arrived, landing], axis=1))
    planes = planes.reshape(capacity, groups, columns + tag * capacity)
    sent = jnp.concatenate(
        [planes[s, :, :columns] for s in range(capacity)]
        + [planes[s, :, columns + s * tag : columns + (s + 1) * tag] for s in range(capacity)],
        axis=1,
    )
    incoming = lax.all_to_all(
        sent[:, None], ROWS, split_axis=0, concat_axis=0, tiled=True
    )[:, 0]
    total = 0.0
    for s in range(capacity):
        spot = capacity * columns + s * tag
        label = incoming[:, spot : spot + 1] - 1.0
        placed = (label.astype(jnp.int32) == index[None, :]).astype(jnp.float32)
        rows = incoming[:, s * columns : (s + 1) * columns]
        total = total + product(placed, rows, ((0,), (0,)))
    return total


def whole_block(mine, first):
    other = lax.ppermute(mine, "core", SWAP)
    both = jnp.stack([jnp.where(first, mine, other), jnp.where(first, other, mine)], axis=1)
    return both.reshape(2 * mine.shape[0] * mine.shape[1], mine.shape[2])


def shards(targets, send_order, send_count, recv_slot, panel, inv_diag):
    sections, block_rows, share = inv_diag.shape
    nx, nz, nc = (lax.axis_size(a) for a in ROWS)
    zi = lax.axis_index("z")
    first = lax.axis_index("core") == 0
    even = zi % 2 == 0
    square = sections * share
    inverse_columns = jnp.swapaxes(inv_diag, 1, 2)

    weight = {}
    names = [(j, k) for j in range(sections) for k in range(j + 1)]
    (tiles,) = pack_tiles(panel, inverse_columns, [names])
    gathered = lax.all_gather(tiles, "z")
    for i, name in enumerate(names):
        weight[name] = gathered[:, i].reshape(nz * share, block_rows)

    residual = redistribute(targets, send_order, send_count, recv_slot)
    columns = residual.shape[1] // 2
    halves = jnp.stack([residual[:square, :columns], residual[:square, columns:]])
    tops = jnp.broadcast_to(halves[None], (nz // 2,) + halves.shape).reshape(nz, square, columns)
    tops = lax.all_to_all(tops, "z", split_axis=0, concat_axis=0, tiled=True)
    pending = [
        tops[:, k * share : (k + 1) * share].reshape(nz * share, columns) for k in range(sections)
    ]
    left, right = residual[square:, :columns], residual[square:, columns:]
    below = [jnp.where(even, left, right), jnp.where(even, right, left)]
    start = ((lax.axis_index("x") * nz + zi) * nc + lax.axis_index("core")) * share
    finished, later = [[], []], []

    def update(side, k, block):
        factor = panel[square:, k * block_rows : (k + 1) * block_rows]
        below[side] = below[side] - product(factor, block)
        finished[side].append(lax.dynamic_slice_in_dim(block, start, share, 0))

    for k in range(sections):
        partial = product(weight[(k, k)], pending[k], ((0,), (0,)))
        partial = partial.reshape(nx * nz, nc, share, columns)
        keep = jnp.where(first, partial[:, 0], partial[:, 1])
        give = jnp.where(first, partial[:, 1], partial[:, 0])
        half = keep + lax.ppermute(give, "core", SWAP)
        copies = jnp.broadcast_to(half[None], (nx,) + half.shape)
        mine = jnp.sum(lax.all_to_all(copies, "x", split_axis=0, concat_axis=0, tiled=True), axis=0)
        solved = whole_block(mine, first)
        for j in range(k + 1, sections):
            pending[j] = pending[j] - product(weight[(j, k)], solved)
        trade = [(i, i ^ 1) for i in range(nz)]
        if k + 1 < sections:
            traded = lax.ppermute(solved, "z", trade)
        else:
            traded = whole_block(lax.ppermute(mine, "z", trade), first)
        update(0, k, solved)
        later.append((k, traded))
        while later and (later[0][0] + 1 <= k or k + 1 == sections):
            old, block = later.pop(0)
            if old < k:
                block = lax.optimization_barrier((mine, block))[1]
            update(1, old, block)
    ends = [jnp.concatenate(finished[h] + [below[h]], axis=0) for h in range(2)]
    return jnp.concatenate(
        [jnp.where(even, ends[0], ends[1]), jnp.where(even, ends[1], ends[0])], axis=1
    )


def solution(mesh):
    ny = mesh.shape["rhs"]
    split = Mesh(mesh.devices.reshape(4, 16, 2, ny), ROWS + ("rhs",))
    placed = (
        P(ROWS + ("rhs",), None),
        P(ROWS),
        P(ROWS, None),
        P(ROWS),
        P(ROWS, None),
        P(None, None, ROWS),
    )
    return jax.shard_map(
        shards, mesh=split, in_specs=placed, out_specs=P(ROWS, "rhs"), check_vma=False
    )
```
